512 devices in a mesh: img: 4 (over x), gs: 128 (over z, y, core).
Axes of the slice: x: 4, y: 4, z: 16, core: 2. Of those that a mesh axis runs over, the one named last changes fastest.
Arguments:
- gaussians: float32 [12288, 10, 128], P('gs'), may hold values from -7.5 to 20, as said below
- target: bfloat16 [4, 128, 4096], P(None, 'img', 'gs'), may hold values from 0 to 1
- request: int32 [4, 128, 8, 3], P('img', 'gs'), may hold values from 0 to 95
- near_counts: int32 [4, 128, 8], P('img', 'gs'), may hold values from 1 to 3, 16 in all within a row
- render_tile: int32 [4, 128, 4], P('img', 'gs'), may hold values from 0 to 511, as said below
- tile_lists: int32 [4, 128, 16], P('img', 'gs'), may hold values from 0 to 15, each once within a row
- tile_counts: int32 [4, 128, 4], P('img', 'gs'), may hold values from 1 to 6, 16 in all within a row
Outputs:
- rendered: bfloat16 [4, 128, 4096], P(None, 'img', 'gs')
- pixel_grad: bfloat16 [4, 128, 4096], P(None, 'img', 'gs')
- gauss_grad: float32 [12288, 10, 128], P('gs')
The draws below stay inside these ranges and needn't reach their ends.
Inputs may be any that keep to these rules, and one draw needn't show every extreme that they name: `gaussians`: value 3 lies in -0.8 to 0.8, values 2 and 4 in 0.02 to 0.8, value 5 in -7.5 to -4.5, values 6 and up in 0 to 1; values 0 and 1 in -4 to 20. `near_counts`: each renderer's row sums to 16. `render_tile`: in each strip every tile number 0 to 511 appears once; render slot j of renderer r draws a tile whose home (number div (4)) is (r + j (128 div (4))) mod 128. `tile_lists`: each renderer's row is a permutation of 0 to 15. `tile_counts`: each renderer's row sums to 16.
All inputs are finite; a program needn't handle non-finite values.
Results may differ from the reference program's by a relative error of at most 0.0024.
Values may be sent and summed in bfloat16 or wider, within the bound.
No kernel may reach another device: no remote copies, remote signals or barrier semaphores. Data moves between devices by JAX's collectives and lax.ppermute only.
A program may use at most 64 MiB of HBM per device.

```python
import math
import jax
import jax.numpy as jnp
import numpy as np
from jax import lax

TILE = 16
BLOCK = 128
CH = 4
TR = 2
TC = 2
SLOTS = 16
NEAR = 8
CAP = 3
KMAX = 6
RADIUS = 5
BLK_DEV = 96
HEIGHT = 128
WIDTH = 4096
N_IMG = 4
N_GS = 128


def spread_log(one_key, shape, lower, upper):
    return jnp.exp(jax.random.uniform(one_key, shape, jnp.float32, jnp.log(lower), jnp.log(upper)))


def draw_gaussians(key, part):
    shape = (BLK_DEV * N_GS, BLOCK)
    keys = jax.random.split(jax.random.fold_in(key, 11), 7)
    centre_x = jax.random.uniform(keys[0], shape, jnp.float32, -4.0, TILE + 4.0)
    centre_y = jax.random.uniform(keys[1], shape, jnp.float32, -4.0, TILE + 4.0)
    correl = jax.random.uniform(keys[4], shape, jnp.float32, -0.8, 0.8)
    conic_a = spread_log(keys[2], shape, 0.02, 0.5)
    conic_c = spread_log(keys[3], shape, 0.02, 0.5)
    logits = jax.random.uniform(keys[5], shape, jnp.float32, -7.5, -4.5)
    shades = jax.random.uniform(keys[6], (CH,) + shape, jnp.float32, 0.0, 1.0)
    columns = [centre_x, centre_y, conic_a, correl, conic_c, logits] + [shades[index] for index in range(CH)]
    return jnp.stack(columns, axis=1)


def draw_render_tile(key, part):
    tiles_dev = TR * TC
    stride = N_GS // tiles_dev

    def one_strip(strip_key):
        home_keys = jax.random.split(strip_key, N_GS)
        offsets = jax.vmap(lambda one_key: jax.random.permutation(one_key, tiles_dev).astype(jnp.int32))(home_keys)
        render_idx = jnp.arange(N_GS, dtype=jnp.int32)[:, None]
        slot_idx = jnp.arange(tiles_dev, dtype=jnp.int32)[None, :]
        home_dev = ((render_idx + slot_idx * stride) % N_GS).astype(jnp.int32)
        local_idx = offsets[home_dev, jnp.broadcast_to(slot_idx, home_dev.shape)]
        return home_dev * tiles_dev + local_idx
    return jax.vmap(one_strip)(jax.random.split(key, N_IMG)).astype(jnp.int32)


def plant(drawn, own_key, low, top_value):
    dims = drawn.shape
    index_at = [jax.random.randint(jax.random.fold_in(own_key, axis), (), 0, dims[axis]) for axis in range(len(dims))]
    drawn = drawn.at[tuple(index_at)].set(low)
    longest = dims.index(max(dims))
    index_at[longest] = (index_at[longest] + 1) % dims[longest]
    return drawn.at[tuple(index_at)].set(top_value)


def block_scale(key, extent, cuts, low, largest):
    def one(dim, blocks):
        heights = jax.random.uniform(jax.random.fold_in(jax.random.fold_in(key, 6), dim), (blocks,), jnp.float32, low / len(cuts), largest / len(cuts))
        return jnp.repeat(jnp.exp(heights), extent[dim] // blocks).reshape((-1,) + (1,) * (len(extent) - dim - 1))

    loudness = one(*cuts[0])
    for cut in cuts[1:]:
        loudness = loudness * one(*cut)
    return loudness


def profile(count, total, reach, lean):
    weights = [(1 << 20) // math.isqrt(standing ** lean) + 1 for standing in range(2, count + 1)]
    spare, holding = total - reach - (count - 1), [1] * (count - 1)
    while spare > 0:
        free = [i for i in range(count - 1) if holding[i] < reach]
        whole, budget = sum([weights[i] for i in free]), spare
        for i in free:
            extra = min(reach - holding[i], max(1, budget * weights[i] // whole), spare)
            holding[i] = holding[i] + extra
            spare = spare - extra
    return np.array([reach] + holding)


def ragged_sizes(key, count, total, bound, slope):
    if count == 2:
        one = jax.random.randint(key, (), max(1, total - bound), min(bound, total - 1) + 1)
        return jnp.stack([one, total - one])
    sizes = jnp.asarray(profile(count, total, bound, slope), jnp.int32)
    pairs = (count - 1) // 2
    donor, taker = sizes[1:1 + 2 * pairs:2], sizes[2:2 + 2 * pairs:2]
    margin = jnp.minimum(donor - 1, bound - taker)
    moved = jax.random.randint(jax.random.fold_in(key, 1), (pairs,), 0, 1 << 20) % (margin + 1)
    sizes = sizes.at[1:1 + 2 * pairs:2].set(donor - moved).at[2:2 + 2 * pairs:2].set(taker + moved)
    return sizes[jax.random.permutation(jax.random.fold_in(key, 2), count)]


def setup_inputs(seed: int = 0) -> dict:
    seeds = jax.random.split(jax.random.key(seed), 8)
    return {
        "gaussians": draw_gaussians(jax.random.fold_in(seeds[7], 71), 0),
        "target": jnp.clip(1.0 * jax.random.uniform(seeds[1], (CH, HEIGHT, WIDTH), jnp.float32) ** block_scale(seeds[1], (CH, HEIGHT, WIDTH), ((1, 4), (2, 128)), -0.2, 0.2), 0.0, 1.0).astype(jnp.bfloat16),
        "request": plant(jax.random.randint(seeds[2], (N_IMG, N_GS, NEAR, CAP), 0, BLK_DEV), jax.random.fold_in(seeds[2], 1), 0, BLK_DEV - 1).astype(jnp.int32),
        "near_counts": jax.vmap(lambda own: ragged_sizes(own, NEAR, SLOTS, CAP, 2))(jax.random.split(seeds[3], N_IMG * N_GS)).reshape((N_IMG, N_GS, NEAR)).astype(jnp.int32),
        "render_tile": draw_render_tile(jax.random.fold_in(seeds[7], 71), 0),
        "tile_lists": jax.vmap(lambda own: jax.random.permutation(own, SLOTS))(jax.random.split(seeds[5], N_IMG * N_GS)).reshape((N_IMG, N_GS, SLOTS)).astype(jnp.int32),
        "tile_counts": jax.vmap(lambda own: ragged_sizes(own, TR * TC, SLOTS, KMAX, 2))(jax.random.split(seeds[6], N_IMG * N_GS)).reshape((N_IMG, N_GS, TR * TC)).astype(jnp.int32),
    }


lam_weight = 0.2
loss_weight = 16.0
sigma_window = 1.5
highest = lax.Precision.HIGHEST

def window_weights(radius):
    offsets = jnp.arange(-radius, radius + 1).astype(jnp.float32)
    weights = jnp.exp(-offsets * offsets / (2.0 * sigma_window * sigma_window))
    return weights / jnp.sum(weights)

def blur_valid(source, radius):
    weights = window_weights(radius)
    col_count = source.shape[2] - 2 * radius
    across = weights[0] * source[:, :, 0:col_count]
    for offset in range(1, 2 * radius + 1):
        across = across + weights[offset] * source[:, :, offset:offset + col_count]
    row_count = source.shape[1] - 2 * radius
    result = weights[0] * across[:, 0:row_count, :]
    for offset in range(1, 2 * radius + 1):
        result = result + weights[offset] * across[:, offset:offset + row_count, :]
    return result

def tile_colour(blocks, live_mask):
    pixel_idx = jnp.arange(TILE * TILE)
    grid_x = (pixel_idx % TILE).astype(jnp.float32) + 0.5
    grid_y = (pixel_idx // TILE).astype(jnp.float32) + 0.5
    mean_x = blocks[:, 0, :].reshape(-1)[:, None]
    mean_y = blocks[:, 1, :].reshape(-1)[:, None]
    conic_a = blocks[:, 2, :].reshape(-1)[:, None]
    correl = blocks[:, 3, :].reshape(-1)[:, None]
    conic_c = blocks[:, 4, :].reshape(-1)[:, None]
    opaque = jax.nn.sigmoid(blocks[:, 5, :]).reshape(-1)[:, None]
    live_rows = jnp.repeat(live_mask, BLOCK)[:, None]
    delta_x = grid_x[None, :] - mean_x
    delta_y = grid_y[None, :] - mean_y
    quadric = conic_a * delta_x * delta_x + 2.0 * correl * jnp.sqrt(conic_a * conic_c) * delta_x * delta_y + conic_c * delta_y * delta_y
    alphas = live_rows * opaque * jnp.exp(-0.5 * quadric)
    log_keep = jnp.log1p(-alphas)
    before = jnp.cumsum(log_keep, axis=0) - log_keep
    weight = jnp.exp(before) * alphas
    shades = jnp.transpose(blocks[:, 6:, :], (1, 0, 2)).reshape(CH, -1)
    return jnp.dot(shades, weight, precision=highest)

def reference(gaussians, target, request, near_counts, render_tile, tile_lists, tile_counts):
    tiles_dev = TR * TC
    strip_col = jnp.arange(N_IMG).astype(jnp.int32)[:, None, None]
    render_col = jnp.arange(N_GS).astype(jnp.int32)[None, :, None]
    near_ends = jnp.cumsum(near_counts, axis=2).astype(jnp.int32)
    near_starts = (near_ends - near_counts).astype(jnp.int32)
    slot_pos = jnp.arange(SLOTS).astype(jnp.int32)
    group_of = lax.optimization_barrier(jnp.sum((slot_pos[None, None, :, None] >= near_ends[:, :, None, :]).astype(jnp.int32), axis=3)).astype(jnp.int32)
    group_start = jnp.take_along_axis(near_starts, group_of, axis=2).astype(jnp.int32)
    place_of = (slot_pos[None, None, :] - group_start).astype(jnp.int32)
    owner_of = ((render_col + group_of - NEAR // 2) % N_GS).astype(jnp.int32)
    local_all = request[strip_col, owner_of, group_of, place_of]
    compact_ids = (owner_of * BLK_DEV + local_all).astype(jnp.int32)
    block_ids = jnp.take_along_axis(compact_ids, tile_lists, axis=2).astype(jnp.int32)
    tile_ends = jnp.cumsum(tile_counts, axis=2).astype(jnp.int32)
    tile_starts = (tile_ends - tile_counts).astype(jnp.int32)
    window_pos = tile_starts[..., None] + jnp.arange(KMAX).astype(jnp.int32)[None, None, None, :]
    live_mask = (window_pos < tile_ends[..., None]).astype(jnp.float32)
    clipped = jnp.minimum(window_pos, SLOTS - 1).astype(jnp.int32)
    tile_ids = block_ids[strip_col[..., None], render_col[..., None], clipped]
    flat_ids = tile_ids.reshape(-1, KMAX).astype(jnp.int32)
    flat_live = live_mask.reshape(-1, KMAX)

    def render_one(packed):
        return tile_colour(gaussians[packed[0]], packed[1])
    colours = lax.map(render_one, (flat_ids, flat_live))
    rounded = colours.astype(jnp.bfloat16).reshape(N_IMG, N_GS, tiles_dev, CH, TILE * TILE)
    home_dev = (render_tile // tiles_dev).astype(jnp.int32)
    local_tile = (render_tile % tiles_dev).astype(jnp.int32)
    canvas = jnp.zeros((N_IMG, N_GS, tiles_dev, CH, TILE * TILE), jnp.bfloat16)
    canvas = canvas.at[strip_col, home_dev, local_tile].set(rounded)
    rendered = canvas.reshape(N_IMG, N_GS, TR, TC, CH, TILE, TILE).transpose(4, 0, 2, 5, 1, 3, 6).reshape(CH, N_IMG * TR * TILE, N_GS * TC * TILE)
    error_map = rendered.astype(jnp.float32) - target.astype(jnp.float32)
    padding = ((0, 0), (RADIUS, RADIUS), (RADIUS, RADIUS))
    smooth = blur_valid(jnp.pad(error_map, padding), RADIUS)
    back_blur = blur_valid(jnp.pad(smooth, padding), RADIUS)
    pixel_grad = (loss_weight * ((1.0 - lam_weight) * error_map + lam_weight * back_blur)).astype(jnp.bfloat16)
    grad_tiles = pixel_grad.reshape(CH, N_IMG, TR, TILE, N_GS, TC, TILE).transpose(1, 4, 2, 5, 0, 3, 6).reshape(N_IMG, N_GS, tiles_dev, CH, TILE * TILE)
    slot_grads = grad_tiles[strip_col, home_dev, local_tile].reshape(-1, CH, TILE * TILE)

    def add_tile(summed, packed):
        ids_here, live_here, cotangent = packed
        picked = gaussians[ids_here]
        unused, pullback = jax.vjp(lambda chosen: tile_colour(chosen, live_here), picked)
        tile_grads, = pullback(cotangent.astype(jnp.float32))
        return (summed.at[ids_here].add(tile_grads), None)
    summed, unused = lax.scan(add_tile, jnp.zeros(gaussians.shape, jnp.float32), (flat_ids, flat_live, slot_grads))
    return (rendered, pixel_grad, summed)
```

```python
import functools
import math

import jax
import jax.numpy as jnp
import numpy as np
from jax import lax
from jax.experimental import pallas as pl
from jax.experimental.pallas import tpu as pltpu
from jax.sharding import Mesh
from jax.sharding import PartitionSpec as P

TILE = 16
BLOCK = 128
CH = 4
SLOTS = 16
NEAR = 8
CAP = 3
RADIUS = 5
TILES = 4
PIX = 256
N_IMG = 4
N_ZQ = 4
N_ZR = 4
N_YC = 8
BLK_DEV = 96
VALS = 10
MSG = 32
SIDE = 32

lam_weight = 0.2
loss_weight = 16.0
sigma_window = 1.5
log2e = math.log2(math.e)

f32 = jnp.float32
bf16 = jnp.bfloat16
highest = lax.Precision.HIGHEST
GS = ("zq", "zr", "yc")

REQ, CNT, REN, LST, TCN, YC, IMG, ZQ, MID = 0, 24, 32, 36, 52, 56, 57, 58, 59


def constants():
    lane = np.arange(128)
    pix = np.arange(PIX)
    x = pix % TILE - 7.5
    y = pix // TILE - 7.5
    moments = np.stack([np.ones(PIX), x, y, x * x, x * y, y * y], axis=1)
    mom = np.zeros((PIX, 32))
    for part in range(3):
        mom[:, part * 8 : part * 8 + 6] = moments
    momt = np.zeros((16, PIX))
    momt[:6] = moments.T
    before = (np.arange(128)[:, None] < np.arange(128)[None, :]).astype(float)
    ones = np.ones((128, 128))
    tri = np.tile(np.concatenate([before, ones], axis=1), (2, 1))
    trib = np.tile(np.concatenate([before.T, ones], axis=1), (2, 1))
    spread = (pix[:, None] % 16 == lane[None, :] % 16).astype(float)
    place = np.zeros((CH, SIDE, 128))
    for c in range(CH):
        for col in range(SIDE):
            place[c, col, (col // 16) * 64 + c * 16 + col % 16] = 1.0
    offsets = np.arange(-RADIUS, RADIUS + 1)
    window = np.exp(-offsets * offsets / (2.0 * sigma_window**2))
    window = window / window.sum()
    rows = N_IMG * SIDE

    def band(count):
        full = np.zeros((count, count))
        for a in range(count):
            for b in range(max(0, a - RADIUS), min(count, a + RADIUS + 1)):
                full[a, b] = window[b - a + RADIUS]
        return full

    vert = band(rows)
    vert = (vert @ vert).reshape(N_IMG, SIDE, rows)
    wide = band(96)
    inner = (wide @ wide)[16:80, 32:64]
    edge = band(64)
    edge = edge @ edge
    left = np.zeros((64, 32))
    left[16:] = edge[:48, :32]
    right = np.zeros((64, 32))
    right[:48] = edge[16:, 32:]
    horiz = np.zeros((3, 256, 128))
    for kind, table in enumerate((inner, left, right)):
        for src in range(64):
            strip = src // 16 - 1
            for c in range(CH):
                if 0 <= strip < 2:
                    row = strip * 64 + c * 16 + src % 16
                elif strip == 2:
                    row = 128 + c * 16 + src % 16
                else:
                    row = 192 + c * 16 + src % 16
                for dst in range(32):
                    horiz[kind, row, (dst // 16) * 64 + c * 16 + dst % 16] = table[src, dst]
    return dict(
        mom=jnp.asarray(mom, bf16),
        momt=jnp.asarray(momt, bf16),
        tri=jnp.asarray(tri, bf16),
        trib=jnp.asarray(trib, bf16),
        spread=jnp.asarray(spread, bf16),
        spreadt=jnp.asarray(spread.T, bf16),
        place=jnp.asarray(place, bf16),
        placet=jnp.asarray(place.transpose(0, 2, 1), bf16),
        vert=jnp.asarray(vert, f32),
        horiz=jnp.asarray(horiz, f32),
    )


def dot(a, b, dims=((1,), (0,)), precision=None):
    return lax.dot_general(a, b, (dims, ((), ())), precision=precision, preferred_element_type=f32)


def halves(value):
    high = value.astype(bf16)
    low = (value - high.astype(f32)).astype(bf16)
    return high, low


def iota(shape, dim):
    return lax.broadcasted_iota(jnp.int32, shape, dim)


def source_places(ints):
    ends = []
    total = 0
    for o in range(NEAR):
        total = total + ints[CNT + o]
        ends.append(total)
    places = []
    for e in range(SLOTS):
        s = ints[LST + e]
        group = 0
        start = 0
        for o in range(NEAR):
            past = s >= ends[o]
            group = group + jnp.where(past, 1, 0)
            start = start + jnp.where(past, ints[CNT + o], 0)
        apart = ints[YC] + group - NEAR // 2
        near = jnp.bitwise_and(apart, 7)
        chunk = jnp.where(apart == near, near, 8 + jnp.bitwise_and(near, 3))
        places.append(chunk * CAP + s - start)
    return places


def list_slots(ints):
    ends = []
    total = 0
    for t in range(TILES - 1):
        total = total + ints[TCN + t]
        ends.append(total)
    slots = []
    for e in range(SLOTS):
        slot = 0
        for t in range(TILES - 1):
            slot = slot + jnp.where(ends[t] <= e, 1, 0)
        slots.append(slot)
    return slots


def pack_kernel(ints, gauss, out):
    lane = iota((1, 128), 1) % 32
    for chunk in range(N_YC):
        group = jnp.bitwise_and(ints[YC] + NEAR // 2 - chunk, 7)
        ids = []
        for c in range(CAP):
            idx = ints[REQ + group * CAP + c]
            out[chunk, 10 * c : 10 * c + 10, :] = gauss[idx]
            ids.append(idx)
        row = jnp.where(lane < 10, ids[0], jnp.where(lane < 20, ids[1], ids[2]))
        out[chunk, 30:32, :] = jnp.broadcast_to(row.astype(f32), (2, 128))


def forward_kernel(ints, own, cross, target, mom, tri, spread, place, payload, raws, pair_w, beta_o,
                   blk, vals, coefs, cols):
    for m in range(12):
        for c in range(CAP):
            src = own[m, 10 * c : 10 * c + 10, :] if m < 8 else cross[m - 8, 10 * c : 10 * c + 10, :]
            blk[m * CAP + c, 0:10, :] = src
    places = source_places(ints)
    slots = list_slots(ints)
    for e in range(SLOTS):
        raw = blk[places[e]]
        raws[e] = raw
        for v in range(6):
            vals[v, e : e + 1, :] = raw[v : v + 1, :]
    mx = vals[0] - 8.0
    my = vals[1] - 8.0
    ca = vals[2]
    cc = vals[4]
    cb = vals[3] * jnp.sqrt(ca * cc)
    logit = vals[5]
    logsig = logit - jnp.log1p(jnp.exp(logit))
    ax = ca * mx + cb * my
    ay = cb * mx + cc * my
    table = [
        log2e * (logsig - 0.5 * (ax * mx + ay * my)),
        log2e * ax,
        log2e * ay,
        (-0.5 * log2e) * ca,
        -log2e * cb,
        (-0.5 * log2e) * cc,
    ]
    coefs[...] = jnp.zeros_like(coefs)
    for k in range(6):
        high = table[k].astype(bf16).astype(f32)
        rest = table[k] - high
        mid = rest.astype(bf16).astype(f32)
        for e in range(SLOTS):
            coefs[e, k : k + 1, :] = high[e : e + 1, :]
            coefs[e, 8 + k : 9 + k, :] = mid[e : e + 1, :]
            coefs[e, 16 + k : 17 + k, :] = (rest - mid)[e : e + 1, :]
    cols[...] = jnp.zeros_like(cols)
    carry = jnp.zeros((PIX, 128), f32)
    for e in range(SLOTS):
        power = dot(mom[...], coefs[e].astype(bf16))
        alpha = jnp.exp2(power)
        lost = alpha * (
            -log2e + alpha * (-log2e / 2 + alpha * (-log2e / 3 + alpha * (-log2e / 4 + alpha * (-log2e / 5))))
        )
        sums = dot(jnp.concatenate(halves(lost), axis=1), tri[...])
        if e:
            carry = jnp.where(slots[e] == slots[e - 1], carry, 0.0)
        weight = jnp.exp2(sums[:, :128] + carry) * alpha
        carry = carry + sums[:, 128:]
        beta_o[e] = alpha * (1.0 + alpha * (1.0 + alpha * (1.0 + alpha * (1.0 + alpha))))
        both = jnp.concatenate(halves(weight), axis=1)
        pair_w[e] = both
        shade_high, shade_low = halves(raws[e, 6:10, :])
        upper = jnp.concatenate([shade_high, shade_high], axis=1)
        lower = jnp.concatenate([shade_low, jnp.zeros_like(shade_low)], axis=1)
        cols[slots[e]] += dot(jnp.concatenate([upper.astype(f32), lower.astype(f32)], axis=0).astype(bf16), both,
                              ((1,), (1,)))
    row_of = iota((TILE, PIX), 1) // TILE == iota((TILE, PIX), 0)
    lane = iota((TILE, 128), 1)
    pieces = []
    for s in range(TILES):
        colour = cols[s]
        colour = colour[0:4, :] + colour[4:8, :]
        for c in range(CH):
            pieces.append(jnp.where(row_of, jnp.broadcast_to(colour[c : c + 1, :], (TILE, PIX)), 0.0))
    laid = dot(jnp.concatenate(pieces, axis=0).astype(bf16), spread[...])
    tiles = []
    for s in range(TILES):
        tile = jnp.zeros((TILE, 128), f32)
        for c in range(CH):
            at = s * 64 + c * 16
            tile = jnp.where((lane // 16) % 4 == c, laid[at : at + 16, :], tile)
        tiles.append(tile)
    goal = jnp.zeros((SIDE, 128), f32)
    for c in range(CH):
        goal = goal + dot(target[c], place[c])
    body = jnp.concatenate(
        [jnp.where(lane < 64, tiles[0], tiles[1]), jnp.where(lane < 64, tiles[2], tiles[3]), goal], axis=0
    ).astype(bf16)
    row = iota((8, 128), 0)
    tags = jnp.zeros((8, 128), jnp.int32)
    for s in range(TILES):
        tags = jnp.where(row == s, jnp.bitwise_and(ints[REN + s], 3), tags)
    tags = tags.astype(f32).astype(bf16)
    for q in range(N_IMG * N_ZQ):
        payload[q, 0:64, :] = body
        payload[q, 64:72, :] = tags


def error_kernel(ints, got, vert, placet, up, err_own, rendered, errs, images):
    lane = iota((TILE, 128), 1)
    half = lane // 64
    halff = half.astype(f32)
    for strip in range(N_IMG):
        for home in range(N_ZQ):
            acc = [jnp.zeros((TILE, 128), f32), jnp.zeros((TILE, 128), f32)]
            for s in range(TILES):
                src = strip * 4 + (home - s) % 4
                both = got[src, 16 * (s // 2) : 16 * (s // 2) + 16, :].astype(f32)
                turned = pltpu.roll(both, 64, 1)
                tile = jnp.where(half == s % 2, both, turned)
                tag = jnp.broadcast_to(got[src, 64:72, :].astype(f32)[s : s + 1, :], (TILE, 128)) - halff
                acc[0] = jnp.where(tag == 0.0, tile, acc[0])
                acc[1] = jnp.where(tag == 2.0, tile, acc[1])
            image = jnp.concatenate(acc, axis=0)
            images[strip * 4 + home] = image
            goal = got[strip * 4 + home, 32:64, :].astype(f32)
            errs[strip * 32 : strip * 32 + 32, home * 128 : home * 128 + 128] = image - goal
    img = ints[IMG]
    blurred = dot(vert[img], errs[...], precision=highest)
    for home in range(N_ZQ):
        up[home] = blurred[:, home * 128 : home * 128 + 128]
        err_own[home] = errs[pl.ds(pl.multiple_of(img * 32, 32), 32), home * 128 : home * 128 + 128]
    mine = images[img * 4 + ints[ZQ]].astype(bf16)
    for c in range(CH):
        rendered[c] = dot(mine, placet[c]).astype(bf16)


def backward_kernel(ints, up, got_mate, got_other, err_own, horiz, placet, spreadt, momt, trib, raws, pair_w,
                    beta_i, own, cross, grad_out, msg_own, msg_cross,
                    ext, back, grads, grow, gcol, vals, sums, blk, pack):
    parity = jnp.bitwise_and(ints[YC], 1)
    place_mid = ints[MID]
    lane32 = iota((SIDE, 128), 1)
    for home in range(N_ZQ):
        at_left = home - jnp.where(place_mid == 0, 1, 0)
        at_right = home + jnp.where(place_mid == 31, 1, 0)
        in_left = at_left >= 0
        in_right = at_right < N_ZQ
        at_left = jnp.maximum(at_left, 0)
        at_right = jnp.minimum(at_right, N_ZQ - 1)
        left = jnp.where(parity == 0, got_other[at_left], got_mate[at_left])
        right = jnp.where(parity == 0, got_mate[at_right], got_other[at_right])
        left = jnp.where(in_left, left, 0.0)
        right = jnp.where(in_right, right, 0.0)
        rows = slice(home * 32, home * 32 + 32)
        ext[rows, 0:128] = up[home]
        ext[rows, 128:256] = jnp.where(lane32 < 64, right, left)
    back[...] = dot(ext[...], horiz[0], precision=highest)

    @pl.when(place_mid == 0)
    def _():
        back[0:32, :] = dot(ext[0:32, :], horiz[1], precision=highest)

    @pl.when(place_mid == 31)
    def _():
        back[96:128, :] = dot(ext[96:128, :], horiz[2], precision=highest)

    for home in range(N_ZQ):
        total = loss_weight * (
            (1.0 - lam_weight) * err_own[home] + lam_weight * back[home * 32 : home * 32 + 32, :]
        )
        grads[home] = total.astype(bf16).astype(f32)
    mine = grads[ints[ZQ]].astype(bf16)
    for c in range(CH):
        grad_out[c] = dot(mine, placet[c]).astype(bf16)

    lane = iota((TILE, 128), 1)
    pieces = []
    for s in range(TILES):
        home = jnp.bitwise_and(ints[ZQ] + s, 3)
        local = jnp.bitwise_and(ints[REN + s], 3)
        down = local // 2
        across = jnp.bitwise_and(local, 1)
        tile = grads[home, pl.ds(pl.multiple_of(down * 16, 16), 16), :]
        for c in range(CH):
            pieces.append(jnp.where(lane // 16 == across * 4 + c, tile, 0.0))
    laid = dot(jnp.concatenate(pieces, axis=0).astype(bf16), spreadt[...])
    row_of = iota((TILE, PIX), 1) // TILE == iota((TILE, PIX), 0)
    for s in range(TILES):
        lines = []
        for c in range(CH):
            at = s * 64 + c * 16
            lines.append(jnp.sum(jnp.where(row_of, laid[at : at + 16, :], 0.0), axis=0, keepdims=True))
        four = jnp.concatenate(lines, axis=0)
        sixteen = jnp.concatenate([four, four, four, jnp.zeros_like(four)], axis=0)
        grow[s] = sixteen.astype(bf16)
        gcol[s] = jnp.transpose(sixteen).astype(bf16)

    slots = list_slots(ints)
    places = source_places(ints)
    carry = jnp.zeros((PIX, 128), f32)
    for e in reversed(range(SLOTS)):
        both = pair_w[e]
        weight = both[:, :128].astype(f32) + both[:, 128:].astype(f32)
        shade = raws[e, 6:10, :]
        high = shade.astype(bf16).astype(f32)
        rest = shade - high
        mid = rest.astype(bf16).astype(f32)
        shades = jnp.concatenate([high, mid, rest - mid, jnp.zeros_like(high)], axis=0).astype(bf16)
        shade_dot = dot(gcol[slots[e]], shades)
        product = weight * shade_dot
        after = dot(jnp.concatenate(halves(product), axis=1), trib[...])
        if e < SLOTS - 1:
            carry = jnp.where(slots[e] == slots[e + 1], carry, 0.0)
        unit = product - (after[:, :128] + carry) * beta_i[e]
        carry = carry + after[:, 128:]
        moment = dot(momt[...], jnp.concatenate(halves(unit), axis=1))
        moment = moment[:, :128] + moment[:, 128:]
        shade_grad = dot(grow[slots[e]], both)
        shade_grad = shade_grad[:, :128] + shade_grad[:, 128:]
        for k in range(6):
            vals[k, e : e + 1, :] = raws[e, k : k + 1, :]
            sums[k, e : e + 1, :] = moment[k : k + 1, :]
        for c in range(CH):
            sums[6 + c, e : e + 1, :] = shade_grad[c : c + 1, :]
    mx = vals[0] - 8.0
    my = vals[1] - 8.0
    ca = vals[2]
    rho = vals[3]
    cc = vals[4]
    opaque = jax.nn.sigmoid(vals[5])
    m0 = -0.5 * sums[0]
    m1 = -0.5 * sums[1]
    m2 = -0.5 * sums[2]
    m3 = -0.5 * sums[3]
    m4 = -0.5 * sums[4]
    m5 = -0.5 * sums[5]
    along_x = m1 - mx * m0
    along_y = m2 - my * m0
    square_x = m3 - 2.0 * mx * m1 + mx * mx * m0
    square_y = m5 - 2.0 * my * m2 + my * my * m0
    mixed = m4 - mx * m2 - my * m1 + mx * my * m0
    root = jnp.sqrt(ca * cc)
    cb = rho * root
    out = [
        -2.0 * (ca * along_x + cb * along_y),
        -2.0 * (cb * along_x + cc * along_y),
        square_x + rho * jnp.sqrt(cc / ca) * mixed,
        2.0 * root * mixed,
        square_y + rho * jnp.sqrt(ca / cc) * mixed,
        (1.0 - opaque) * sums[0],
    ] + [sums[6 + c] for c in range(CH)]
    blk[...] = jnp.zeros_like(blk)
    for e in range(SLOTS):
        for v in range(VALS):
            blk[places[e], v : v + 1, :] = out[v][e : e + 1, :]
    lane1 = iota((2, 128), 1)
    group = jnp.where(lane1 // 32 == jnp.bitwise_and(ints[YC], 3), 1.0, 0.0)
    for m in range(12):
        for c in range(CAP):
            pack[m, 10 * c : 10 * c + 10, :] = blk[m * CAP + c, 0:10, :]
        ids = own[m, 30:32, :] if m < 8 else cross[m - 8, 30:32, :]
        pack[m, 30:32, :] = ids * group
    msg_own[...] = pack[0:8].astype(bf16)
    msg_cross[...] = pack[8:12].astype(bf16)


def collect_kernel(got, out):
    lane = iota((1, 128), 1)
    line = lane % 32
    value = jnp.where(line < 10, line, jnp.where(line < 20, line - 10, line - 20))
    goals = []
    for quad in range(8):
        ids = jnp.zeros((1, 128), f32)
        for m in range(4):
            ids = ids + got[quad * 4 + m, 16:32, :].astype(f32)[14:15, :]
        goals.append(jnp.where(line < 30, ids.astype(jnp.int32) * 16 + value, -1))
    flat = got[...].reshape(32 * MSG, 128)
    rows = 384
    for part in range(BLK_DEV * 16 // rows):
        here = iota((rows, 128), 0) + part * rows
        hits = [jnp.where(here == goal, 1.0, 0.0).astype(bf16) for goal in goals]
        total = dot(jnp.concatenate(hits, axis=1), flat)
        out[part * 24 : part * 24 + 24] = total.reshape(24, 16, 128)[:, :VALS, :]


VM = pl.BlockSpec(memory_space=pltpu.VMEM)
SM = pl.BlockSpec(memory_space=pltpu.SMEM)


def call(kernel, outs, scratch, n_in, name, flops=0):
    return pl.pallas_call(
        kernel,
        out_shape=tuple(jax.ShapeDtypeStruct(shape, dtype) for shape, dtype in outs),
        in_specs=[SM] + [VM] * (n_in - 1) if name != "collect" else [VM] * n_in,
        out_specs=tuple(VM for _ in outs),
        scratch_shapes=[pltpu.VMEM(shape, dtype) for shape, dtype in scratch],
        name=name,
    )


def on_device(gaussians, target, request, near_counts, render_tile, tile_lists, tile_counts):
    table = constants()
    yc = lax.axis_index("yc")
    img = lax.axis_index("img")
    zq = lax.axis_index("zq")
    mid = lax.axis_index("zr") * N_YC + yc
    ints = jnp.concatenate(
        [
            request.reshape(24),
            near_counts.reshape(8),
            render_tile.reshape(4),
            tile_lists.reshape(16),
            tile_counts.reshape(4),
            jnp.stack([yc, img, zq, mid, yc, yc, yc, yc]).astype(jnp.int32),
        ]
    )
    n_gs = N_ZQ * N_ZR * N_YC
    up_route = []
    for r in range(n_gs):
        j = r % N_YC
        if j < 4:
            up_route.append((r, (r + N_YC) % n_gs))
        elif j > 4:
            up_route.append((r, (r - N_YC) % n_gs))
    back_route = [(b, a) for a, b in up_route]

    (sent,) = call(pack_kernel, [((N_YC, MSG, 128), f32)], [], 2, "pack")(ints, gaussians)
    own = lax.all_to_all(sent, "yc", 0, 0, tiled=True)
    crossing = jnp.where(yc < 4, own[4:8], own[0:4])
    cross = lax.ppermute(crossing, GS, up_route)

    payload, raws, pair_w, beta = call(
        forward_kernel,
        [
            ((N_IMG * N_ZQ, 72, 128), bf16),
            ((SLOTS, 16, 128), f32),
            ((SLOTS, PIX, 256), bf16),
            ((SLOTS, PIX, 128), f32),
        ],
        [((36, 16, 128), f32), ((6, 16, 128), f32), ((SLOTS, 32, 128), f32), ((TILES, 8, PIX), f32)],
        8,
        "forward",
    )(ints, own, cross, target, table["mom"], table["tri"], table["spread"], table["place"])
    got = lax.all_to_all(payload, ("img", "zq"), 0, 0, tiled=True)

    up, err_own, rendered = call(
        error_kernel,
        [((N_ZQ, SIDE, 128), f32), ((N_ZQ, SIDE, 128), f32), ((CH, SIDE, SIDE), bf16)],
        [((N_IMG * SIDE, 512), f32), ((16, SIDE, 128), f32)],
        4,
        "error",
    )(ints, got, table["vert"], table["placet"])

    other = [((2 * c - 1) % n_gs, 2 * c) for c in range(n_gs // 2)]
    other = other + [(b, a) for a, b in other]
    got_other = lax.ppermute(up, GS, other)
    got_mate = lax.ppermute(up, GS, [(r, r ^ 1) for r in range(n_gs)])

    pixel_grad, msg_own, msg_cross = call(
        backward_kernel,
        [((CH, SIDE, SIDE), bf16), ((N_YC, MSG, 128), bf16), ((4, MSG, 128), bf16)],
        [
            ((128, 256), f32),
            ((128, 128), f32),
            ((N_ZQ, SIDE, 128), f32),
            ((TILES, 16, PIX), bf16),
            ((TILES, PIX, 16), bf16),
            ((6, 16, 128), f32),
            ((10, 16, 128), f32),
            ((36, 16, 128), f32),
            ((12, MSG, 128), f32),
        ],
        15,
        "backward",
    )(
        ints, up, got_mate, got_other, err_own, table["horiz"], table["placet"], table["spreadt"], table["momt"],
        table["trib"], raws, pair_w, beta, own, cross,
    )
    returned = lax.ppermute(msg_cross, GS, back_route)
    apart = jnp.arange(N_YC) + NEAR // 2 - yc
    straight = ((apart >= 0) & (apart < NEAR))[:, None, None]
    merged = jnp.where(straight, msg_own, jnp.concatenate([returned, returned], axis=0))
    spread_out = jnp.broadcast_to(merged[None], (N_IMG, N_YC, MSG, 128)).reshape(N_IMG * N_YC, MSG, 128)
    all_msgs = lax.all_to_all(spread_out, ("img", "yc"), 0, 0, tiled=True)
    (summed,) = call(collect_kernel, [((BLK_DEV, VALS, 128), f32)], [], 1, "collect")(all_msgs)
    return (rendered, pixel_grad, summed)


def solution(mesh):
    wide = Mesh(mesh.devices.reshape(N_IMG, N_ZQ, N_ZR, N_YC), ("img", "zq", "zr", "yc"))
    in_specs = (
        P(GS, None, None),
        P(None, "img", GS),
        P("img", GS, None, None),
        P("img", GS, None),
        P("img", GS, None),
        P("img", GS, None),
        P("img", GS, None),
    )
    out_specs = (P(None, "img", GS), P(None, "img", GS), P(GS, None, None))
    return jax.shard_map(on_device, mesh=wide, in_specs=in_specs, out_specs=out_specs, check_vma=False)
```

```python
import functools
import math

import jax
import jax.numpy as jnp
import numpy as np
from jax import lax
from jax.experimental import pallas as pl
from jax.experimental.pallas import tpu as pltpu
from jax.sharding import Mesh
from jax.sharding import PartitionSpec as P

TILE = 16
BLOCK = 128
CH = 4
SLOTS = 16
PAIRS = SLOTS // 2
NEAR = 8
CAP = 3
RADIUS = 5
TILES = 4
PIX = 256
N_IMG = 4
N_ZQ = 4
N_ZR = 4
N_YC = 8
BLK_DEV = 96
VALS = 10
MSG = 32
SIDE = 32

lam_weight = 0.2
loss_weight = 16.0
sigma_window = 1.5
log2e = math.log2(math.e)

f32 = jnp.float32
bf16 = jnp.bfloat16
highest = lax.Precision.HIGHEST
GS = ("zq", "zr", "yc")


def constants():
    lane = np.arange(128)
    pix = np.arange(PIX)
    x = pix % TILE - 7.5
    y = pix // TILE - 7.5
    moments = np.stack([np.ones(PIX), x, y, x * x, x * y, y * y], axis=1)
    mom = np.zeros((PIX, 32))
    for part in range(3):
        mom[:, part * 8 : part * 8 + 6] = moments
    momt = np.zeros((16, PIX))
    momt[:6] = moments.T
    long = (np.arange(256)[:, None] < np.arange(256)[None, :]).astype(float)
    alone = long * (np.arange(256)[:, None] // 128 == np.arange(256)[None, :] // 128)
    tri = np.stack([alone, long])
    trib = np.stack([alone.T, long.T])
    spread = (pix[:, None] % 16 == lane[None, :] % 16).astype(float)
    place = np.zeros((CH, SIDE, 128))
    for c in range(CH):
        for col in range(SIDE):
            place[c, col, (col // 16) * 64 + c * 16 + col % 16] = 1.0
    offsets = np.arange(-RADIUS, RADIUS + 1)
    window = np.exp(-offsets * offsets / (2.0 * sigma_window**2))
    window = window / window.sum()
    rows = N_IMG * SIDE

    def band(count):
        full = np.zeros((count, count))
        for a in range(count):
            for b in range(max(0, a - RADIUS), min(count, a + RADIUS + 1)):
                full[a, b] = window[b - a + RADIUS]
        return full

    vert = band(rows)
    vert = (vert @ vert).reshape(N_IMG, SIDE, rows)
    wide = band(96)
    inner = (wide @ wide)[16:80, 32:64]
    edge = band(64)
    edge = edge @ edge
    left = np.zeros((64, 32))
    left[16:] = edge[:48, :32]
    right = np.zeros((64, 32))
    right[:48] = edge[16:, 32:]
    horiz = np.zeros((3, 256, 128))
    for kind, table in enumerate((inner, left, right)):
        for src in range(64):
            strip = src // 16 - 1
            for c in range(CH):
                if 0 <= strip < 2:
                    row = strip * 64 + c * 16 + src % 16
                elif strip == 2:
                    row = 128 + c * 16 + src % 16
                else:
                    row = 192 + c * 16 + src % 16
                for dst in range(32):
                    horiz[kind, row, (dst // 16) * 64 + c * 16 + dst % 16] = table[src, dst]
    return dict(
        mom=jnp.asarray(mom, bf16),
        momt=jnp.asarray(momt, bf16),
        tri=jnp.asarray(tri, bf16),
        trib=jnp.asarray(trib, bf16),
        spread=jnp.asarray(spread, bf16),
        spreadt=jnp.asarray(spread.T, bf16),
        place=jnp.asarray(place, bf16),
        placet=jnp.asarray(place.transpose(0, 2, 1), bf16),
        vert=jnp.asarray(vert, f32),
        horiz=jnp.asarray(horiz, f32),
    )


def dot(a, b, dims=((1,), (0,)), precision=None):
    return lax.dot_general(a, b, (dims, ((), ())), precision=precision, preferred_element_type=f32)


def halves(value):
    high = value.astype(bf16)
    low = (value - high.astype(f32)).astype(bf16)
    return high, low


def iota(shape, dim):
    return lax.broadcasted_iota(jnp.int32, shape, dim)


def source_places(counts, lists, yc):
    ends = []
    total = 0
    for o in range(NEAR):
        total = total + counts[o]
        ends.append(total)
    places = []
    for e in range(SLOTS):
        s = lists[e]
        group = 0
        start = 0
        for o in range(NEAR):
            past = s >= ends[o]
            group = group + jnp.where(past, 1, 0)
            start = start + jnp.where(past, counts[o], 0)
        apart = yc + group - NEAR // 2
        near = jnp.bitwise_and(apart, 7)
        chunk = jnp.where(apart == near, near, 8 + jnp.bitwise_and(near, 3))
        places.append(chunk * CAP + s - start)
    return places


def list_slots(tile_counts):
    ends = []
    total = 0
    for t in range(TILES - 1):
        total = total + tile_counts[t]
        ends.append(total)
    slots = []
    for e in range(SLOTS):
        slot = 0
        for t in range(TILES - 1):
            slot = slot + jnp.where(ends[t] <= e, 1, 0)
        slots.append(slot)
    return slots


def pack_kernel(request, gauss, out):
    yc = lax.axis_index("yc")
    lane = iota((1, 128), 1) % 32
    for chunk in range(N_YC):
        group = jnp.bitwise_and(yc + NEAR // 2 - chunk, 7)
        ids = []
        for c in range(CAP):
            idx = request[c, 0, group]
            for v in range(VALS):
                out[chunk, 10 * c + v : 10 * c + v + 1, :] = gauss[v, pl.ds(idx, 1), :]
            ids.append(idx)
        row = jnp.where(lane < 10, ids[0], jnp.where(lane < 20, ids[1], ids[2]))
        out[chunk, 30:32, :] = jnp.broadcast_to(row.astype(f32), (2, 128))


def forward_kernel(counts, lists, tile_counts, render, own, cross, target, mom, tri, spread, place,
                   payload, raws, pair_o, beta_o, blk, vals, coefs, shades, cols, pair_w, beta, sems):
    for m in range(12):
        for c in range(CAP):
            src = own[m, 10 * c : 10 * c + 10, :] if m < 8 else cross[m - 8, 10 * c : 10 * c + 10, :]
            blk[m * CAP + c, 0:10, :] = src
    places = source_places(counts, lists, lax.axis_index("yc"))
    slots = list_slots(tile_counts)
    shades[...] = jnp.zeros_like(shades)
    for e in range(SLOTS):
        raw = blk[places[e]]
        raws[e] = raw
        for v in range(6):
            vals[v, e : e + 1, :] = raw[v : v + 1, :]
        shade = raw[6:10, :]
        high = shade.astype(bf16).astype(f32)
        at = 4 * (e % 2)
        lanes = slice(128 * (e % 2), 128 * (e % 2) + 128)
        shades[e // 2, at : at + 4, lanes] = high
        shades[e // 2, 8 + at : 12 + at, lanes] = shade - high
    mx = vals[0] - 8.0
    my = vals[1] - 8.0
    ca = vals[2]
    cc = vals[4]
    cb = vals[3] * jnp.sqrt(ca * cc)
    logit = vals[5]
    logsig = logit - jnp.log1p(jnp.exp(logit))
    ax = ca * mx + cb * my
    ay = cb * mx + cc * my
    table = [
        log2e * (logsig - 0.5 * (ax * mx + ay * my)),
        log2e * ax,
        log2e * ay,
        (-0.5 * log2e) * ca,
        -log2e * cb,
        (-0.5 * log2e) * cc,
    ]
    coefs[...] = jnp.zeros_like(coefs)
    for k in range(6):
        high = table[k].astype(bf16).astype(f32)
        rest = table[k] - high
        mid = rest.astype(bf16).astype(f32)
        for e in range(SLOTS):
            lanes = slice(128 * (e % 2), 128 * (e % 2) + 128)
            coefs[e // 2, k : k + 1, lanes] = high[e : e + 1, :]
            coefs[e // 2, 8 + k : 9 + k, lanes] = mid[e : e + 1, :]
            coefs[e // 2, 16 + k : 17 + k, lanes] = (rest - mid)[e : e + 1, :]
    cols[...] = jnp.zeros_like(cols)
    upper = iota((8, PIX), 0) < 4
    carry = jnp.zeros((PIX, 128), f32)
    for pair in range(PAIRS):
        first, second = 2 * pair, 2 * pair + 1
        same = slots[first] == slots[second]
        alpha = jnp.exp2(dot(mom[...], coefs[pair].astype(bf16)))
        lost = alpha * (-1.0 + alpha * (-1.0 / 2 + alpha * (-1.0 / 3 + alpha * (-1.0 / 4))))
        beta[pair] = (alpha * jnp.exp(-lost)).astype(bf16)
        sums = dot(lost.astype(bf16), tri[jnp.where(same, 1, 0)])
        whole = jnp.broadcast_to(sums[:, 255:256] + lost[:, 255:256], (PIX, 128))
        if pair:
            carry = jnp.where(slots[first] == slots[first - 1], carry, 0.0)
        later = jnp.where(same, carry, 0.0)
        weight = (jnp.exp(sums + jnp.concatenate([carry, later], axis=1)) * alpha).astype(bf16)
        carry = whole + later
        pair_w[pair] = weight
        colour = dot(shades[pair].astype(bf16), weight, ((1,), (1,)))
        colour = colour[0:8, :] + colour[8:16, :]
        cols[slots[first]] += jnp.where(upper, colour, 0.0)
        cols[slots[second]] += jnp.where(upper, 0.0, colour)
    copies = (
        pltpu.make_async_copy(pair_w, pair_o, sems.at[0]),
        pltpu.make_async_copy(beta, beta_o, sems.at[1]),
    )
    for copy in copies:
        copy.start()
    row_of = iota((TILE, PIX), 1) // TILE == iota((TILE, PIX), 0)
    lane = iota((TILE, 128), 1)
    pieces = []
    for s in range(TILES):
        colour = cols[s]
        colour = colour[0:4, :] + colour[4:8, :]
        for c in range(CH):
            pieces.append(jnp.where(row_of, jnp.broadcast_to(colour[c : c + 1, :], (TILE, PIX)), 0.0))
    laid = dot(jnp.concatenate(pieces, axis=0).astype(bf16), spread[...])
    tiles = []
    for s in range(TILES):
        tile = jnp.zeros((TILE, 128), f32)
        for c in range(CH):
            at = s * 64 + c * 16
            tile = jnp.where((lane // 16) % 4 == c, laid[at : at + 16, :], tile)
        tiles.append(tile)
    goal = jnp.zeros((SIDE, 128), f32)
    for c in range(CH):
        goal = goal + dot(target[c], place[c])
    body = jnp.concatenate(
        [jnp.where(lane < 64, tiles[0], tiles[1]), jnp.where(lane < 64, tiles[2], tiles[3]), goal], axis=0
    ).astype(bf16)
    row = iota((8, 128), 0)
    tags = jnp.zeros((8, 128), jnp.int32)
    for s in range(TILES):
        tags = jnp.where(row == s, jnp.bitwise_and(render[s], 3), tags)
    tags = tags.astype(f32).astype(bf16)
    for q in range(N_IMG * N_ZQ):
        payload[q, 0:64, :] = body
        payload[q, 64:72, :] = tags
    for copy in copies:
        copy.wait()


def error_kernel(got, vert, placet, up, err_own, rendered, errs, images):
    lane = iota((TILE, 128), 1)
    half = lane // 64
    halff = half.astype(f32)
    for strip in range(N_IMG):
        for home in range(N_ZQ):
            acc = [jnp.zeros((TILE, 128), f32), jnp.zeros((TILE, 128), f32)]
            for s in range(TILES):
                src = strip * 4 + (home - s) % 4
                both = got[src, 16 * (s // 2) : 16 * (s // 2) + 16, :].astype(f32)
                turned = pltpu.roll(both, 64, 1)
                tile = jnp.where(half == s % 2, both, turned)
                tag = jnp.broadcast_to(got[src, 64:72, :].astype(f32)[s : s + 1, :], (TILE, 128)) - halff
                acc[0] = jnp.where(tag == 0.0, tile, acc[0])
                acc[1] = jnp.where(tag == 2.0, tile, acc[1])
            image = jnp.concatenate(acc, axis=0)
            images[strip * 4 + home] = image
            goal = got[strip * 4 + home, 32:64, :].astype(f32)
            errs[strip * 32 : strip * 32 + 32, home * 128 : home * 128 + 128] = image - goal
    img = lax.axis_index("img")
    blurred = dot(vert[img], errs[...], precision=highest)
    for home in range(N_ZQ):
        up[home] = blurred[:, home * 128 : home * 128 + 128]
        err_own[home] = errs[pl.ds(pl.multiple_of(img * 32, 32), 32), home * 128 : home * 128 + 128]
    mine = images[img * 4 + lax.axis_index("zq")].astype(bf16)
    for c in range(CH):
        rendered[c] = dot(mine, placet[c]).astype(bf16)


def backward_kernel(counts, lists, tile_counts, render, up, got_mate, got_other, err_own, horiz, placet, spreadt,
                    momt, trib, raws, pair_o, beta_o, own, cross, grad_out, msg_own, msg_cross,
                    ext, back, grads, vals, sums, blk, pack, shades, shade_sums, pair_w, beta, sems):
    copies = (
        pltpu.make_async_copy(pair_o, pair_w, sems.at[0]),
        pltpu.make_async_copy(beta_o, beta, sems.at[1]),
    )
    for copy in copies:
        copy.start()
    yc = lax.axis_index("yc")
    zq = lax.axis_index("zq")
    parity = jnp.bitwise_and(yc, 1)
    place_mid = lax.axis_index("zr") * N_YC + yc
    lane32 = iota((SIDE, 128), 1)
    for home in range(N_ZQ):
        at_left = home - jnp.where(place_mid == 0, 1, 0)
        at_right = home + jnp.where(place_mid == 31, 1, 0)
        in_left = at_left >= 0
        in_right = at_right < N_ZQ
        at_left = jnp.maximum(at_left, 0)
        at_right = jnp.minimum(at_right, N_ZQ - 1)
        left = jnp.where(parity == 0, got_other[at_left], got_mate[at_left])
        right = jnp.where(parity == 0, got_mate[at_right], got_other[at_right])
        left = jnp.where(in_left, left, 0.0)
        right = jnp.where(in_right, right, 0.0)
        rows = slice(home * 32, home * 32 + 32)
        ext[rows, 0:128] = up[home]
        ext[rows, 128:256] = jnp.where(lane32 < 64, right, left)
    back[...] = dot(ext[...], horiz[0], precision=highest)

    @pl.when(place_mid == 0)
    def _():
        back[0:32, :] = dot(ext[0:32, :], horiz[1], precision=highest)

    @pl.when(place_mid == 31)
    def _():
        back[96:128, :] = dot(ext[96:128, :], horiz[2], precision=highest)

    for home in range(N_ZQ):
        total = loss_weight * (
            (1.0 - lam_weight) * err_own[home] + lam_weight * back[home * 32 : home * 32 + 32, :]
        )
        grads[home] = total.astype(bf16).astype(f32)
    mine = grads[zq].astype(bf16)
    for c in range(CH):
        grad_out[c] = dot(mine, placet[c]).astype(bf16)

    lane = iota((TILE, 128), 1)
    pieces = []
    for s in range(TILES):
        home = jnp.bitwise_and(zq + s, 3)
        local = jnp.bitwise_and(render[s], 3)
        down = local // 2
        across = jnp.bitwise_and(local, 1)
        tile = grads[home, pl.ds(pl.multiple_of(down * 16, 16), 16), :]
        for c in range(CH):
            pieces.append(jnp.where(lane // 16 == across * 4 + c, tile, 0.0))
    laid = dot(jnp.concatenate(pieces, axis=0).astype(bf16), spreadt[...])
    row_of = iota((TILE, PIX), 1) // TILE == iota((TILE, PIX), 0)
    lines = []
    for s in range(TILES):
        four = []
        for c in range(CH):
            at = s * 64 + c * 16
            four.append(jnp.sum(jnp.where(row_of, laid[at : at + 16, :], 0.0), axis=0, keepdims=True))
        lines = lines + four + four
    grad_rows = jnp.concatenate(lines, axis=0)
    grad_cols = jnp.transpose(grad_rows).astype(bf16)
    grad_rows = grad_rows.astype(bf16)

    slots = list_slots(tile_counts)
    places = source_places(counts, lists, yc)
    shades[...] = jnp.zeros_like(shades)
    for e in range(SLOTS):
        shade = raws[e, 6:10, :]
        high = shade.astype(bf16).astype(f32)
        at = pl.ds(pl.multiple_of(slots[e] * 8, 8), 8)
        shades[e // 2, at, 128 * (e % 2) : 128 * (e % 2) + 128] = jnp.concatenate([high, shade - high], axis=0)
        for k in range(6):
            vals[k, e : e + 1, :] = raws[e, k : k + 1, :]
    for copy in copies:
        copy.wait()
    carry = jnp.zeros((PIX, 128), f32)
    for pair in reversed(range(PAIRS)):
        first, second = 2 * pair, 2 * pair + 1
        same = slots[first] == slots[second]
        product = pair_w[pair].astype(f32) * dot(grad_cols, shades[pair].astype(bf16))
        after = dot(product.astype(bf16), trib[jnp.where(same, 1, 0)])
        whole = jnp.broadcast_to(after[:, 0:1] + product[:, 0:1], (PIX, 128))
        if pair < PAIRS - 1:
            carry = jnp.where(slots[second] == slots[second + 1], carry, 0.0)
        earlier = jnp.where(same, carry, 0.0)
        unit = product - (after + jnp.concatenate([earlier, carry], axis=1)) * beta[pair].astype(f32)
        carry = whole + earlier
        high, low = halves(unit)
        moment = dot(momt[...], high) + dot(momt[...], low)
        shade_grad = dot(grad_rows, pair_w[pair])
        for s in range(TILES):
            shade_sums[pair, s] = shade_grad[8 * s : 8 * s + 8, :]
        for k in range(6):
            sums[k, first : first + 1, :] = moment[k : k + 1, :128]
            sums[k, second : second + 1, :] = moment[k : k + 1, 128:]
    for e in range(SLOTS):
        shade_grad = shade_sums[e // 2, slots[e]]
        for c in range(CH):
            sums[6 + c, e : e + 1, :] = shade_grad[c : c + 1, 128 * (e % 2) : 128 * (e % 2) + 128]
    mx = vals[0] - 8.0
    my = vals[1] - 8.0
    ca = vals[2]
    rho = vals[3]
    cc = vals[4]
    opaque = jax.nn.sigmoid(vals[5])
    m0 = -0.5 * sums[0]
    m1 = -0.5 * sums[1]
    m2 = -0.5 * sums[2]
    m3 = -0.5 * sums[3]
    m4 = -0.5 * sums[4]
    m5 = -0.5 * sums[5]
    along_x = m1 - mx * m0
    along_y = m2 - my * m0
    square_x = m3 - 2.0 * mx * m1 + mx * mx * m0
    square_y = m5 - 2.0 * my * m2 + my * my * m0
    mixed = m4 - mx * m2 - my * m1 + mx * my * m0
    root = jnp.sqrt(ca * cc)
    cb = rho * root
    out = [
        -2.0 * (ca * along_x + cb * along_y),
        -2.0 * (cb * along_x + cc * along_y),
        square_x + rho * jnp.sqrt(cc / ca) * mixed,
        2.0 * root * mixed,
        square_y + rho * jnp.sqrt(ca / cc) * mixed,
        (1.0 - opaque) * sums[0],
    ] + [sums[6 + c] for c in range(CH)]
    blk[...] = jnp.zeros_like(blk)
    for e in range(SLOTS):
        for v in range(VALS):
            blk[places[e], v : v + 1, :] = out[v][e : e + 1, :]
    lane1 = iota((2, 128), 1)
    group = jnp.where(lane1 // 32 == jnp.bitwise_and(yc, 3), 1.0, 0.0)
    for m in range(12):
        for c in range(CAP):
            pack[m, 10 * c : 10 * c + 10, :] = blk[m * CAP + c, 0:10, :]
        ids = own[m, 30:32, :] if m < 8 else cross[m - 8, 30:32, :]
        pack[m, 30:32, :] = ids * group
    msg_own[...] = pack[0:8].astype(bf16)
    msg_cross[...] = pack[8:12].astype(bf16)


def collect_kernel(got, out):
    lane = iota((1, 128), 1)
    line = lane % 32
    value = jnp.where(line < 10, line, jnp.where(line < 20, line - 10, line - 20))
    goals = []
    for quad in range(8):
        ids = jnp.zeros((1, 128), f32)
        for m in range(4):
            ids = ids + got[quad * 4 + m, 16:32, :].astype(f32)[14:15, :]
        goals.append(jnp.where(line < 30, ids.astype(jnp.int32) + value * BLK_DEV, -1))
    flat = got[...].reshape(32 * MSG, 128)
    rows = 2 * BLK_DEV
    for part in range(VALS // 2):
        here = iota((rows, 128), 0) + part * rows
        hits = [jnp.where(here == goal, 1.0, 0.0).astype(bf16) for goal in goals]
        total = dot(jnp.concatenate(hits, axis=1), flat)
        out[2 * part] = total[:BLK_DEV]
        out[2 * part + 1] = total[BLK_DEV:]


VM = pl.BlockSpec(memory_space=pltpu.VMEM)
SM = pl.BlockSpec(memory_space=pltpu.SMEM)
ANY = pl.BlockSpec(memory_space=pl.ANY)


def call(kernel, ins, outs, scratch, name, limit=16):
    return pl.pallas_call(
        kernel,
        out_shape=tuple(jax.ShapeDtypeStruct(shape, dtype) for shape, dtype, _ in outs),
        in_specs=ins,
        out_specs=tuple(space for _, _, space in outs),
        scratch_shapes=scratch,
        compiler_params=pltpu.CompilerParams(vmem_limit_bytes=limit << 20 if limit else None),
        name=name,
    )


def on_device(gaussians, target, request, near_counts, render_tile, tile_lists, tile_counts):
    table = constants()
    yc = lax.axis_index("yc")
    counts = near_counts.reshape(NEAR)
    render = render_tile.reshape(TILES)
    lists = tile_lists.reshape(SLOTS)
    lengths = tile_counts.reshape(TILES)
    wanted = request.transpose(0, 3, 1, 2).reshape(CAP, 1, NEAR)
    n_gs = N_ZQ * N_ZR * N_YC
    up_route = []
    for r in range(n_gs):
        j = r % N_YC
        if j < 4:
            up_route.append((r, (r + N_YC) % n_gs))
        elif j > 4:
            up_route.append((r, (r - N_YC) % n_gs))
    back_route = [(b, a) for a, b in up_route]
    group = N_IMG * N_ZQ
    vm = pltpu.VMEM

    (sent,) = call(pack_kernel, [SM, VM], [((N_YC, MSG, 128), f32, VM)], [], "pack", None)(
        wanted, gaussians.transpose(1, 0, 2)
    )
    own = lax.all_to_all(sent, "yc", 0, 0, tiled=True)
    crossing = jnp.where(yc < 4, own[4:8], own[0:4])
    cross = lax.ppermute(crossing, GS, up_route)

    payload, raws, pair_w, beta = call(
        forward_kernel,
        [SM] * 4 + [VM] * 7,
        [
            ((group, 72, 128), bf16, VM),
            ((SLOTS, 16, 128), f32, VM),
            ((PAIRS, PIX, 256), bf16, ANY),
            ((PAIRS, PIX, 256), bf16, ANY),
        ],
        [
            vm((36, 16, 128), f32),
            vm((6, 16, 128), f32),
            vm((PAIRS, 32, 256), f32),
            vm((PAIRS, 16, 256), f32),
            vm((TILES, 8, PIX), f32),
            vm((PAIRS, PIX, 256), bf16),
            vm((PAIRS, PIX, 256), bf16),
            pltpu.SemaphoreType.DMA((2,)),
        ],
        "forward",
        None,
    )(
        counts, lists, lengths, render, own, cross, target, table["mom"], table["tri"], table["spread"],
        table["place"],
    )
    got = lax.all_to_all(payload, ("img", "zq"), 0, 0, tiled=True)

    up, err_own, rendered = call(
        error_kernel,
        [VM] * 3,
        [((N_ZQ, SIDE, 128), f32, VM), ((N_ZQ, SIDE, 128), f32, VM), ((CH, SIDE, SIDE), bf16, VM)],
        [vm((N_IMG * SIDE, 512), f32), vm((16, SIDE, 128), f32)],
        "error",
    )(got, table["vert"], table["placet"])

    other = [((2 * c - 1) % n_gs, 2 * c) for c in range(n_gs // 2)]
    other = other + [(b, a) for a, b in other]
    got_other = lax.ppermute(up, GS, other)
    got_mate = lax.ppermute(up, GS, [(r, r ^ 1) for r in range(n_gs)])

    pixel_grad, msg_own, msg_cross = call(
        backward_kernel,
        [SM] * 4 + [VM] * 10 + [ANY] * 2 + [VM] * 2,
        [((CH, SIDE, SIDE), bf16, VM), ((N_YC, MSG, 128), bf16, VM), ((4, MSG, 128), bf16, VM)],
        [
            vm((128, 256), f32),
            vm((128, 128), f32),
            vm((N_ZQ, SIDE, 128), f32),
            vm((6, 16, 128), f32),
            vm((10, 16, 128), f32),
            vm((36, 16, 128), f32),
            vm((12, MSG, 128), f32),
            vm((PAIRS, 32, 256), f32),
            vm((PAIRS, TILES, 8, 256), f32),
            vm((PAIRS, PIX, 256), bf16),
            vm((PAIRS, PIX, 256), bf16),
            pltpu.SemaphoreType.DMA((2,)),
        ],
        "backward",
        None,
    )(
        counts, lists, lengths, render, up, got_mate, got_other, err_own, table["horiz"], table["placet"],
        table["spreadt"], table["momt"], table["trib"], raws, pair_w, beta, own, cross,
    )
    returned = lax.ppermute(msg_cross, GS, back_route)
    apart = jnp.arange(N_YC) + NEAR // 2 - yc
    straight = ((apart >= 0) & (apart < NEAR))[:, None, None]
    merged = jnp.where(straight, msg_own, jnp.concatenate([returned, returned], axis=0))
    spread_out = jnp.broadcast_to(merged[None], (N_IMG, N_YC, MSG, 128)).reshape(N_IMG * N_YC, MSG, 128)
    all_msgs = lax.all_to_all(spread_out, ("img", "yc"), 0, 0, tiled=True)
    (summed,) = call(collect_kernel, [VM], [((VALS, BLK_DEV, 128), f32, VM)], [], "collect")(all_msgs)
    return (rendered, pixel_grad, summed.transpose(1, 0, 2))


def solution(mesh):
    wide = Mesh(mesh.devices.reshape(N_IMG, N_ZQ, N_ZR, N_YC), ("img", "zq", "zr", "yc"))
    in_specs = (
        P(GS, None, None),
        P(None, "img", GS),
        P("img", GS, None, None),
        P("img", GS, None),
        P("img", GS, None),
        P("img", GS, None),
        P("img", GS, None),
    )
    out_specs = (P(None, "img", GS), P(None, "img", GS), P(GS, None, None))
    return jax.shard_map(on_device, mesh=wide, in_specs=in_specs, out_specs=out_specs, check_vma=False)
```

```python
import functools
import math

import jax
import jax.numpy as jnp
import numpy as np
from jax import lax
from jax.experimental import pallas as pl
from jax.experimental.pallas import tpu as pltpu
from jax.sharding import Mesh
from jax.sharding import PartitionSpec as P

TILE = 16
BLOCK = 128
CH = 4
SLOTS = 16
PAIRS = SLOTS // 2
NEAR = 8
CAP = 3
RADIUS = 5
KMAX = 6
TILES = 4
PIX = 256
N_IMG = 4
N_ZQ = 4
N_ZR = 4
N_YC = 8
BLK_DEV = 96
VALS = 10
MSG = 32
SIDE = 32

lam_weight = 0.2
loss_weight = 16.0
sigma_window = 1.5
log2e = math.log2(math.e)

f32 = jnp.float32
bf16 = jnp.bfloat16
highest = lax.Precision.HIGHEST
GS = ("zq", "zr", "yc")

CNT, LST, TCN, REN = 0, 8, 24, 28


def constants():
    lane = np.arange(128)
    pix = np.arange(PIX)
    x = pix % TILE - 7.5
    y = pix // TILE - 7.5
    moments = np.stack([np.ones(PIX), x, y, x * x, x * y, y * y], axis=1)
    mom = np.zeros((PIX, 32))
    for part in range(3):
        mom[:, part * 8 : part * 8 + 6] = moments
    momt = np.zeros((16, PIX))
    momt[:6] = moments.T
    long = (np.arange(256)[:, None] < np.arange(256)[None, :]).astype(float)
    alone = long * (np.arange(256)[:, None] // 128 == np.arange(256)[None, :] // 128)
    tri = -np.stack([alone, long])
    trib = np.stack([alone.T, long.T])
    spread = (pix[:, None] % 16 == lane[None, :] % 16).astype(float)
    place = np.zeros((CH, SIDE, 128))
    for c in range(CH):
        for col in range(SIDE):
            place[c, col, (col // 16) * 64 + c * 16 + col % 16] = 1.0
    offsets = np.arange(-RADIUS, RADIUS + 1)
    window = np.exp(-offsets * offsets / (2.0 * sigma_window**2))
    window = window / window.sum()
    rows = N_IMG * SIDE

    def band(count):
        full = np.zeros((count, count))
        for a in range(count):
            for b in range(max(0, a - RADIUS), min(count, a + RADIUS + 1)):
                full[a, b] = window[b - a + RADIUS]
        return full

    vert = band(rows)
    vert = (vert @ vert).reshape(N_IMG, SIDE, rows)
    wide = band(96)
    inner = (wide @ wide)[16:80, 32:64]
    edge = band(64)
    edge = edge @ edge
    left = np.zeros((64, 32))
    left[16:] = edge[:48, :32]
    right = np.zeros((64, 32))
    right[:48] = edge[16:, 32:]
    horiz = np.zeros((3, 256, 128))
    for kind, table in enumerate((inner, left, right)):
        for src in range(64):
            strip = src // 16 - 1
            for c in range(CH):
                if 0 <= strip < 2:
                    row = strip * 64 + c * 16 + src % 16
                elif strip == 2:
                    row = 128 + c * 16 + src % 16
                else:
                    row = 192 + c * 16 + src % 16
                for dst in range(32):
                    horiz[kind, row, (dst // 16) * 64 + c * 16 + dst % 16] = table[src, dst]
    return dict(
        mom=jnp.asarray(mom, bf16),
        momt=jnp.asarray(momt, bf16),
        tri=jnp.asarray(tri, bf16),
        trib=jnp.asarray(trib, bf16),
        spread=jnp.asarray(spread, bf16),
        spreadt=jnp.asarray(spread.T, bf16),
        place=jnp.asarray(place, bf16),
        placet=jnp.asarray(place.transpose(0, 2, 1), bf16),
        vert=jnp.asarray(vert, f32),
        horiz=jnp.asarray(horiz, f32),
    )


def dot(a, b, dims=((1,), (0,)), precision=None):
    return lax.dot_general(a, b, (dims, ((), ())), precision=precision, preferred_element_type=f32)


def halves(value):
    high = value.astype(bf16)
    low = (value - high.astype(f32)).astype(bf16)
    return high, low


def iota(shape, dim):
    return lax.broadcasted_iota(jnp.int32, shape, dim)


def source_places(ints, table, yc):
    start = jnp.int32(0)
    for o in range(NEAR):
        apart = yc + o - NEAR // 2
        near = jnp.bitwise_and(apart, 7)
        base = CAP * jnp.where(apart == near, near, 8 + jnp.bitwise_and(near, 3))
        for c in range(CAP):
            table[start + c] = base + c
        start = start + ints[CNT + o]
    return [table[ints[LST + e]] for e in range(SLOTS)]


def list_slots(ints, table):
    start = jnp.int32(0)
    for t in range(TILES):
        for c in range(KMAX):
            table[start + c] = jnp.int32(t)
        start = start + ints[TCN + t]
    return [table[e] for e in range(SLOTS)]


def fetch(pairs, sems):
    copies = [pltpu.make_async_copy(src, dst, sems.at[n]) for n, (src, dst) in enumerate(pairs)]
    for copy in copies:
        copy.start()
    return copies


def wait(copies):
    for copy in copies:
        copy.wait()


def pack_kernel(request_in, gauss_in, out, request, gauss, sems):
    wait(fetch([(request_in, request), (gauss_in, gauss)], sems))
    yc = lax.axis_index("yc")
    lane = iota((1, 128), 1) % 32
    for chunk in range(N_YC):
        group = jnp.bitwise_and(yc + NEAR // 2 - chunk, 7)
        ids = []
        for c in range(CAP):
            idx = request[c, 0, group]
            for v in range(VALS):
                out[chunk, 10 * c + v : 10 * c + v + 1, :] = gauss[v, pl.ds(idx, 1), :]
            ids.append(idx)
        row = jnp.where(lane < 10, ids[0], jnp.where(lane < 20, ids[1], ids[2]))
        out[chunk, 30:32, :] = jnp.broadcast_to(row.astype(f32), (2, 128))


def forward_kernel(ints_in, target_in, mom_in, tri_in, spread_in, place_in, own, cross, payload, raws, pair_o,
                   beta_o, ints, group_table, slot_table, target, mom, tri, spread, place, blk, vals, coefs, shades, cols, pair_w, beta, in_sems, sems):
    loads = fetch(
        [
            (ints_in, ints),
            (mom_in, mom), (tri_in, tri), (spread_in, spread), (place_in, place), (target_in, target),
        ],
        in_sems,
    )
    for m in range(12):
        for c in range(CAP):
            src = own[m, 10 * c : 10 * c + 10, :] if m < 8 else cross[m - 8, 10 * c : 10 * c + 10, :]
            blk[m * CAP + c, 0:10, :] = src
    coefs[...] = jnp.zeros_like(coefs)
    cols[...] = jnp.zeros_like(cols)
    wait(loads[:1])
    places = source_places(ints, group_table, lax.axis_index("yc"))
    slots = list_slots(ints, slot_table)
    shades[...] = jnp.zeros_like(shades)
    for e in range(SLOTS):
        raw = blk[places[e]]
        raws[e] = raw
        for v in range(6):
            vals[v, e : e + 1, :] = raw[v : v + 1, :]
        shade = raw[6:10, :]
        high = shade.astype(bf16).astype(f32)
        at = 4 * (e % 2)
        lanes = slice(128 * (e % 2), 128 * (e % 2) + 128)
        shades[e // 2, at : at + 4, lanes] = high
        shades[e // 2, 8 + at : 12 + at, lanes] = shade - high
    mx = vals[0] - 8.0
    my = vals[1] - 8.0
    ca = vals[2]
    cc = vals[4]
    cb = vals[3] * jnp.sqrt(ca * cc)
    logit = vals[5]
    logsig = logit - jnp.log1p(jnp.exp(logit))
    ax = ca * mx + cb * my
    ay = cb * mx + cc * my
    table = [
        log2e * (logsig - 0.5 * (ax * mx + ay * my)),
        log2e * ax,
        log2e * ay,
        (-0.5 * log2e) * ca,
        -log2e * cb,
        (-0.5 * log2e) * cc,
    ]
    for k in range(6):
        high = table[k].astype(bf16).astype(f32)
        rest = table[k] - high
        mid = rest.astype(bf16).astype(f32)
        for e in range(SLOTS):
            lanes = slice(128 * (e % 2), 128 * (e % 2) + 128)
            coefs[e // 2, k : k + 1, lanes] = high[e : e + 1, :]
            coefs[e // 2, 8 + k : 9 + k, lanes] = mid[e : e + 1, :]
            coefs[e // 2, 16 + k : 17 + k, lanes] = (rest - mid)[e : e + 1, :]
    wait(loads[1:])
    upper = iota((8, PIX), 0) < 4
    carry = jnp.zeros((PIX, 128), f32)
    for pair in range(PAIRS):
        first, second = 2 * pair, 2 * pair + 1
        same = slots[first] == slots[second]
        alpha = jnp.exp2(dot(mom[...], coefs[pair].astype(bf16)))
        lost = alpha * (log2e + alpha * (log2e / 2 + alpha * (log2e / 3 + alpha * (log2e / 4))))
        beta[pair] = (alpha * jnp.exp2(lost)).astype(bf16)
        sums = dot(lost.astype(bf16), tri[jnp.where(same, 1, 0)])
        whole = jnp.broadcast_to(sums[:, 255:256] - lost[:, 255:256], (PIX, 128))
        if pair:
            carry = jnp.where(slots[first] == slots[first - 1], carry, 0.0)
        later = jnp.where(same, carry, 0.0)
        weight = (jnp.exp2(sums + jnp.concatenate([carry, later], axis=1)) * alpha).astype(bf16)
        carry = whole + later
        pair_w[pair] = weight
        colour = dot(shades[pair].astype(bf16), weight, ((1,), (1,)))
        colour = colour[0:8, :] + colour[8:16, :]
        cols[slots[first]] += jnp.where(upper, colour, 0.0)
        cols[slots[second]] += jnp.where(upper, 0.0, colour)
    copies = (
        pltpu.make_async_copy(pair_w, pair_o, sems.at[0]),
        pltpu.make_async_copy(beta, beta_o, sems.at[1]),
    )
    for copy in copies:
        copy.start()
    row_of = iota((TILE, PIX), 1) // TILE == iota((TILE, PIX), 0)
    lane = iota((TILE, 128), 1)
    pieces = []
    for s in range(TILES):
        colour = cols[s]
        colour = colour[0:4, :] + colour[4:8, :]
        for c in range(CH):
            pieces.append(jnp.where(row_of, jnp.broadcast_to(colour[c : c + 1, :], (TILE, PIX)), 0.0))
    laid = dot(jnp.concatenate(pieces, axis=0).astype(bf16), spread[...])
    tiles = []
    for s in range(TILES):
        tile = jnp.zeros((TILE, 128), f32)
        for c in range(CH):
            at = s * 64 + c * 16
            tile = jnp.where((lane // 16) % 4 == c, laid[at : at + 16, :], tile)
        tiles.append(tile)
    goal = jnp.zeros((SIDE, 128), f32)
    for c in range(CH):
        goal = goal + dot(target[c], place[c])
    body = jnp.concatenate(
        [jnp.where(lane < 64, tiles[0], tiles[1]), jnp.where(lane < 64, tiles[2], tiles[3]), goal], axis=0
    ).astype(bf16)
    row = iota((8, 128), 0)
    tags = jnp.zeros((8, 128), jnp.int32)
    for s in range(TILES):
        tags = jnp.where(row == s, jnp.bitwise_and(ints[REN + s], 3), tags)
    tags = tags.astype(f32).astype(bf16)
    for q in range(N_IMG * N_ZQ):
        payload[q, 0:64, :] = body
        payload[q, 64:72, :] = tags
    for copy in copies:
        copy.wait()


def error_kernel(got, vert, placet, up, edge, err_own, rendered, errs, images):
    lane = iota((TILE, 128), 1)
    half = lane // 64
    halff = half.astype(f32)
    for strip in range(N_IMG):
        for home in range(N_ZQ):
            acc = [jnp.zeros((TILE, 128), f32), jnp.zeros((TILE, 128), f32)]
            for s in range(TILES):
                src = strip * 4 + (home - s) % 4
                both = got[src, 16 * (s // 2) : 16 * (s // 2) + 16, :].astype(f32)
                turned = pltpu.roll(both, 64, 1)
                tile = jnp.where(half == s % 2, both, turned)
                tag = jnp.broadcast_to(got[src, 64:72, :].astype(f32)[s : s + 1, :], (TILE, 128)) - halff
                acc[0] = jnp.where(tag == 0.0, tile, acc[0])
                acc[1] = jnp.where(tag == 2.0, tile, acc[1])
            image = jnp.concatenate(acc, axis=0)
            images[strip * 4 + home] = image
            goal = got[strip * 4 + home, 32:64, :].astype(f32)
            errs[strip * 32 : strip * 32 + 32, home * 128 : home * 128 + 128] = image - goal
    img = lax.axis_index("img")
    blurred = dot(vert[img], errs[...], precision=highest)
    for home in range(N_ZQ):
        up[home] = blurred[:, home * 128 : home * 128 + 128]
        edge[home] = blurred[:, home * 128 : home * 128 + 128].astype(bf16)
        err_own[home] = errs[pl.ds(pl.multiple_of(img * 32, 32), 32), home * 128 : home * 128 + 128]
    mine = images[img * 4 + lax.axis_index("zq")].astype(bf16)
    for c in range(CH):
        rendered[c] = dot(mine, placet[c]).astype(bf16)


def backward_kernel(ints_in, horiz_in, placet_in, spreadt_in, momt_in, trib_in,
                    pair_o, beta_o, up, got_mate, got_other, err_own, raws, own, cross,
                    grad_out, msg_own, msg_cross,
                    ints, group_table, slot_table, horiz, placet, spreadt, momt, trib, pair_w, beta,
                    ext, back, grads, vals, sums, blk, pack, shades, shade_sums, sems):
    loads = fetch(
        [
            (ints_in, ints),
            (horiz_in, horiz), (placet_in, placet), (spreadt_in, spreadt), (momt_in, momt), (trib_in, trib),
            (pair_o, pair_w), (beta_o, beta),
        ],
        sems,
    )
    yc = lax.axis_index("yc")
    zq = lax.axis_index("zq")
    parity = jnp.bitwise_and(yc, 1)
    place_mid = lax.axis_index("zr") * N_YC + yc
    lane32 = iota((SIDE, 128), 1)
    for home in range(N_ZQ):
        at_left = home - jnp.where(place_mid == 0, 1, 0)
        at_right = home + jnp.where(place_mid == 31, 1, 0)
        in_left = at_left >= 0
        in_right = at_right < N_ZQ
        at_left = jnp.maximum(at_left, 0)
        at_right = jnp.minimum(at_right, N_ZQ - 1)
        left = jnp.where(parity == 0, got_other[at_left], got_mate[at_left])
        right = jnp.where(parity == 0, got_mate[at_right], got_other[at_right])
        left = jnp.where(in_left, left.astype(f32), 0.0)
        right = jnp.where(in_right, right.astype(f32), 0.0)
        rows = slice(home * 32, home * 32 + 32)
        ext[rows, 0:128] = up[home]
        ext[rows, 128:256] = jnp.where(lane32 < 64, right, left)
    wait(loads[:4])
    back[...] = dot(ext[...], horiz[0], precision=highest)

    @pl.when(place_mid == 0)
    def _():
        back[0:32, :] = dot(ext[0:32, :], horiz[1], precision=highest)

    @pl.when(place_mid == 31)
    def _():
        back[96:128, :] = dot(ext[96:128, :], horiz[2], precision=highest)

    for home in range(N_ZQ):
        total = loss_weight * (
            (1.0 - lam_weight) * err_own[home] + lam_weight * back[home * 32 : home * 32 + 32, :]
        )
        grads[home] = total.astype(bf16).astype(f32)
    mine = grads[zq].astype(bf16)
    for c in range(CH):
        grad_out[c] = dot(mine, placet[c]).astype(bf16)

    lane = iota((TILE, 128), 1)
    pieces = []
    for s in range(TILES):
        home = jnp.bitwise_and(zq + s, 3)
        local = jnp.bitwise_and(ints[REN + s], 3)
        down = local // 2
        across = jnp.bitwise_and(local, 1)
        tile = grads[home, pl.ds(pl.multiple_of(down * 16, 16), 16), :]
        for c in range(CH):
            pieces.append(jnp.where(lane // 16 == across * 4 + c, tile, 0.0))
    laid = dot(jnp.concatenate(pieces, axis=0).astype(bf16), spreadt[...])
    row_of = iota((TILE, PIX), 1) // TILE == iota((TILE, PIX), 0)
    lines = []
    for s in range(TILES):
        four = []
        for c in range(CH):
            at = s * 64 + c * 16
            four.append(jnp.sum(jnp.where(row_of, laid[at : at + 16, :], 0.0), axis=0, keepdims=True))
        lines = lines + four + four
    grad_rows = jnp.concatenate(lines, axis=0)
    grad_cols = jnp.transpose(grad_rows).astype(bf16)
    grad_rows = grad_rows.astype(bf16)

    slots = list_slots(ints, slot_table)
    places = source_places(ints, group_table, yc)
    shades[...] = jnp.zeros_like(shades)
    for e in range(SLOTS):
        shade = raws[e, 6:10, :]
        high = shade.astype(bf16).astype(f32)
        at = pl.ds(pl.multiple_of(slots[e] * 8, 8), 8)
        shades[e // 2, at, 128 * (e % 2) : 128 * (e % 2) + 128] = jnp.concatenate([high, shade - high], axis=0)
        for k in range(6):
            vals[k, e : e + 1, :] = raws[e, k : k + 1, :]
    wait(loads[4:])
    carry = jnp.zeros((PIX, 128), f32)
    for pair in reversed(range(PAIRS)):
        first, second = 2 * pair, 2 * pair + 1
        same = slots[first] == slots[second]
        product = pair_w[pair].astype(f32) * dot(grad_cols, shades[pair].astype(bf16))
        after = dot(product.astype(bf16), trib[jnp.where(same, 1, 0)])
        whole = jnp.broadcast_to(after[:, 0:1] + product[:, 0:1], (PIX, 128))
        if pair < PAIRS - 1:
            carry = jnp.where(slots[second] == slots[second + 1], carry, 0.0)
        earlier = jnp.where(same, carry, 0.0)
        unit = product - (after + jnp.concatenate([earlier, carry], axis=1)) * beta[pair].astype(f32)
        carry = whole + earlier
        high, low = halves(unit)
        moment = dot(momt[...], high) + dot(momt[...], low)
        shade_grad = dot(grad_rows, pair_w[pair])
        for s in range(TILES):
            shade_sums[pair, s] = shade_grad[8 * s : 8 * s + 8, :]
        for k in range(6):
            sums[k, first : first + 1, :] = moment[k : k + 1, :128]
            sums[k, second : second + 1, :] = moment[k : k + 1, 128:]
    for e in range(SLOTS):
        shade_grad = shade_sums[e // 2, slots[e]]
        for c in range(CH):
            sums[6 + c, e : e + 1, :] = shade_grad[c : c + 1, 128 * (e % 2) : 128 * (e % 2) + 128]
    mx = vals[0] - 8.0
    my = vals[1] - 8.0
    ca = vals[2]
    rho = vals[3]
    cc = vals[4]
    opaque = jax.nn.sigmoid(vals[5])
    m0 = -0.5 * sums[0]
    m1 = -0.5 * sums[1]
    m2 = -0.5 * sums[2]
    m3 = -0.5 * sums[3]
    m4 = -0.5 * sums[4]
    m5 = -0.5 * sums[5]
    along_x = m1 - mx * m0
    along_y = m2 - my * m0
    square_x = m3 - 2.0 * mx * m1 + mx * mx * m0
    square_y = m5 - 2.0 * my * m2 + my * my * m0
    mixed = m4 - mx * m2 - my * m1 + mx * my * m0
    root = jnp.sqrt(ca * cc)
    cb = rho * root
    out = [
        -2.0 * (ca * along_x + cb * along_y),
        -2.0 * (cb * along_x + cc * along_y),
        square_x + rho * jnp.sqrt(cc / ca) * mixed,
        2.0 * root * mixed,
        square_y + rho * jnp.sqrt(ca / cc) * mixed,
        (1.0 - opaque) * sums[0],
    ] + [sums[6 + c] for c in range(CH)]
    blk[...] = jnp.zeros_like(blk)
    for e in range(SLOTS):
        for v in range(VALS):
            blk[places[e], v : v + 1, :] = out[v][e : e + 1, :]
    lane1 = iota((2, 128), 1)
    group = jnp.where(lane1 // 32 == jnp.bitwise_and(yc, 3), 1.0, 0.0)
    for m in range(12):
        for c in range(CAP):
            pack[m, 10 * c : 10 * c + 10, :] = blk[m * CAP + c, 0:10, :]
        ids = own[m, 30:32, :] if m < 8 else cross[m - 8, 30:32, :]
        pack[m, 30:32, :] = ids * group
    msg_own[...] = pack[0:8].astype(bf16)
    msg_cross[...] = pack[8:12].astype(bf16)


def collect_kernel(got, out):
    lane = iota((1, 128), 1)
    line = lane % 32
    value = jnp.where(line < 10, line, jnp.where(line < 20, line - 10, line - 20))
    goals = []
    for quad in range(8):
        ids = jnp.zeros((1, 128), f32)
        for m in range(4):
            ids = ids + got[quad * 4 + m, 16:32, :].astype(f32)[14:15, :]
        goals.append(jnp.where(line < 30, ids.astype(jnp.int32) + value * BLK_DEV, -1))
    flat = got[...].reshape(32 * MSG, 128)
    rows = 2 * BLK_DEV
    for part in range(VALS // 2):
        here = iota((rows, 128), 0) + part * rows
        hits = [jnp.where(here == goal, 1.0, 0.0).astype(bf16) for goal in goals]
        total = dot(jnp.concatenate(hits, axis=1), flat)
        out[2 * part] = total[:BLK_DEV]
        out[2 * part + 1] = total[BLK_DEV:]


VM = pl.BlockSpec(memory_space=pltpu.VMEM)
SM = pl.BlockSpec(memory_space=pltpu.SMEM)
HB = pl.BlockSpec(memory_space=pltpu.HBM)


def call(kernel, ins, outs, scratch, name, limit=16):
    return pl.pallas_call(
        kernel,
        out_shape=tuple(jax.ShapeDtypeStruct(shape, dtype) for shape, dtype, _ in outs),
        in_specs=ins,
        out_specs=tuple(space for _, _, space in outs),
        scratch_shapes=scratch,
        compiler_params=pltpu.CompilerParams(vmem_limit_bytes=limit << 20 if limit else None),
        name=name,
    )


def on_device(gaussians, target, request, near_counts, render_tile, tile_lists, tile_counts):
    table = constants()
    yc = lax.axis_index("yc")
    ints = jnp.concatenate(
        [near_counts.reshape(NEAR), tile_lists.reshape(SLOTS), tile_counts.reshape(TILES), render_tile.reshape(TILES)]
    )
    wanted = request.transpose(0, 3, 1, 2).reshape(CAP, 1, NEAR)
    n_gs = N_ZQ * N_ZR * N_YC
    up_route = []
    for r in range(n_gs):
        j = r % N_YC
        if j < 4:
            up_route.append((r, (r + N_YC) % n_gs))
        elif j > 4:
            up_route.append((r, (r - N_YC) % n_gs))
    back_route = [(b, a) for a, b in up_route]
    group = N_IMG * N_ZQ
    vm = pltpu.VMEM

    small = [pltpu.SMEM((32,), jnp.int32) for _ in range(3)]
    dma = pltpu.SemaphoreType.DMA

    (sent,) = call(
        pack_kernel,
        [HB, HB],
        [((N_YC, MSG, 128), f32, VM)],
        [pltpu.SMEM((CAP, 1, NEAR), jnp.int32), vm((VALS, BLK_DEV, 128), f32), dma((2,))],
        "pack",
        None,
    )(wanted, gaussians.transpose(1, 0, 2))
    own = lax.all_to_all(sent, "yc", 0, 0, tiled=True)
    crossing = jnp.where(yc < 4, own[4:8], own[0:4])
    cross = lax.ppermute(crossing, GS, up_route)

    payload, raws, pair_w, beta = call(
        forward_kernel,
        [HB] * 6 + [VM] * 2,
        [
            ((group, 72, 128), bf16, VM),
            ((SLOTS, 16, 128), f32, VM),
            ((PAIRS, PIX, 256), bf16, HB),
            ((PAIRS, PIX, 256), bf16, HB),
        ],
        small
        + [
            vm((CH, SIDE, SIDE), bf16),
            vm((PIX, 32), bf16),
            vm((2, 256, 256), bf16),
            vm((PIX, 128), bf16),
            vm((CH, SIDE, 128), bf16),
            vm((36, 16, 128), f32),
            vm((6, 16, 128), f32),
            vm((PAIRS, 32, 256), f32),
            vm((PAIRS, 16, 256), f32),
            vm((TILES, 8, PIX), f32),
            vm((PAIRS, PIX, 256), bf16),
            vm((PAIRS, PIX, 256), bf16),
            dma((6,)),
            dma((2,)),
        ],
        "forward",
    )(
        ints, target, table["mom"], table["tri"], table["spread"], table["place"],
        own, cross,
    )
    got = lax.all_to_all(payload, ("img", "zq"), 0, 0, tiled=True)

    up, edge, err_own, rendered = call(
        error_kernel,
        [VM] * 3,
        [
            ((N_ZQ, SIDE, 128), f32, VM),
            ((N_ZQ, SIDE, 128), bf16, VM),
            ((N_ZQ, SIDE, 128), f32, VM),
            ((CH, SIDE, SIDE), bf16, VM),
        ],
        [vm((N_IMG * SIDE, 512), f32), vm((16, SIDE, 128), f32)],
        "error",
    )(got, table["vert"], table["placet"])

    other = [((2 * c - 1) % n_gs, 2 * c) for c in range(n_gs // 2)]
    other = other + [(b, a) for a, b in other]
    got_other = lax.ppermute(edge, GS, other)
    got_mate = lax.ppermute(edge, GS, [(r, r ^ 1) for r in range(n_gs)])

    pixel_grad, msg_own, msg_cross = call(
        backward_kernel,
        [HB] * 8 + [VM] * 7,
        [((CH, SIDE, SIDE), bf16, VM), ((N_YC, MSG, 128), bf16, VM), ((4, MSG, 128), bf16, VM)],
        small
        + [
            vm((3, 256, 128), f32),
            vm((CH, 128, SIDE), bf16),
            vm((128, PIX), bf16),
            vm((16, PIX), bf16),
            vm((2, 256, 256), bf16),
            vm((PAIRS, PIX, 256), bf16),
            vm((PAIRS, PIX, 256), bf16),
            vm((128, 256), f32),
            vm((128, 128), f32),
            vm((N_ZQ, SIDE, 128), f32),
            vm((6, 16, 128), f32),
            vm((10, 16, 128), f32),
            vm((36, 16, 128), f32),
            vm((12, MSG, 128), f32),
            vm((PAIRS, 32, 256), f32),
            vm((PAIRS, TILES, 8, 256), f32),
            dma((8,)),
        ],
        "backward",
    )(
        ints, table["horiz"], table["placet"], table["spreadt"], table["momt"],
        table["trib"], pair_w, beta, up, got_mate, got_other, err_own, raws, own, cross,
    )
    returned = lax.ppermute(msg_cross, GS, back_route)
    apart = jnp.arange(N_YC) + NEAR // 2 - yc
    straight = ((apart >= 0) & (apart < NEAR))[:, None, None]
    merged = jnp.where(straight, msg_own, jnp.concatenate([returned, returned], axis=0))
    spread_out = jnp.broadcast_to(merged[None], (N_IMG, N_YC, MSG, 128)).reshape(N_IMG * N_YC, MSG, 128)
    all_msgs = lax.all_to_all(spread_out, ("img", "yc"), 0, 0, tiled=True)
    (summed,) = call(collect_kernel, [VM], [((VALS, BLK_DEV, 128), f32, VM)], [], "collect")(all_msgs)
    return (rendered, pixel_grad, summed.transpose(1, 0, 2))


def solution(mesh):
    wide = Mesh(mesh.devices.reshape(N_IMG, N_ZQ, N_ZR, N_YC), ("img", "zq", "zr", "yc"))
    in_specs = (
        P(GS, None, None),
        P(None, "img", GS),
        P("img", GS, None, None),
        P("img", GS, None),
        P("img", GS, None),
        P("img", GS, None),
        P("img", GS, None),
    )
    out_specs = (P(None, "img", GS), P(None, "img", GS), P(GS, None, None))
    return jax.shard_map(on_device, mesh=wide, in_specs=in_specs, out_specs=out_specs, check_vma=False)
```

```python
import functools
import math

import jax
import jax.numpy as jnp
import numpy as np
from jax import lax
from jax.experimental import pallas as pl
from jax.experimental.pallas import tpu as pltpu
from jax.sharding import Mesh
from jax.sharding import PartitionSpec as P

TILE = 16
BLOCK = 128
CH = 4
SLOTS = 16
PAIRS = SLOTS // 2
NEAR = 8
CAP = 3
RADIUS = 5
KMAX = 6
TILES = 4
PIX = 256
N_IMG = 4
N_ZQ = 4
N_ZR = 4
N_YC = 8
BLK_DEV = 96
VALS = 10
MSG = 32
SIDE = 32

lam_weight = 0.2
loss_weight = 16.0
sigma_window = 1.5
log2e = math.log2(math.e)

f32 = jnp.float32
bf16 = jnp.bfloat16
GS = ("zq", "zr", "yc")

CNT, LST, TCN, REN = 0, 8, 24, 28


def constants():
    lane = np.arange(128)
    pix = np.arange(PIX)
    x = pix % TILE - 7.5
    y = pix // TILE - 7.5
    moments = np.stack([np.ones(PIX), x, y, x * x, x * y, y * y], axis=1)
    mom = np.zeros((PIX, 32))
    for part in range(3):
        mom[:, part * 8 : part * 8 + 6] = moments
    momt = np.zeros((16, PIX))
    momt[:6] = moments.T
    long = (np.arange(256)[:, None] < np.arange(256)[None, :]).astype(float)
    alone = long * (np.arange(256)[:, None] // 128 == np.arange(256)[None, :] // 128)
    tri = -np.stack([alone, long])
    trib = np.stack([alone.T, long.T])
    spread = (pix[:, None] % 16 == lane[None, :] % 16).astype(float)
    place = np.zeros((CH, SIDE, 128))
    for c in range(CH):
        for col in range(SIDE):
            place[c, col, (col // 16) * 64 + c * 16 + col % 16] = 1.0
    offsets = np.arange(-RADIUS, RADIUS + 1)
    window = np.exp(-offsets * offsets / (2.0 * sigma_window**2))
    window = window / window.sum()
    rows = N_IMG * SIDE

    def band(count):
        full = np.zeros((count, count))
        for a in range(count):
            for b in range(max(0, a - RADIUS), min(count, a + RADIUS + 1)):
                full[a, b] = window[b - a + RADIUS]
        return full

    vert = band(rows)
    vert = (vert @ vert).reshape(N_IMG, SIDE, rows)
    wide = band(96)
    inner = (wide @ wide)[16:80, 32:64]
    edge = band(64)
    edge = edge @ edge
    left = np.zeros((64, 32))
    left[16:] = edge[:48, :32]
    right = np.zeros((64, 32))
    right[:48] = edge[16:, 32:]
    horiz = np.zeros((3, 256, 128))
    for kind, table in enumerate((inner, left, right)):
        for src in range(64):
            strip = src // 16 - 1
            for c in range(CH):
                if 0 <= strip < 2:
                    row = strip * 64 + c * 16 + src % 16
                elif strip == 2:
                    row = 128 + c * 16 + src % 16
                else:
                    row = 192 + c * 16 + src % 16
                for dst in range(32):
                    horiz[kind, row, (dst // 16) * 64 + c * 16 + dst % 16] = table[src, dst]
    return dict(
        mom=jnp.asarray(mom, bf16),
        momt=jnp.asarray(momt, bf16),
        tri=jnp.asarray(tri, bf16),
        trib=jnp.asarray(trib, bf16),
        spread=jnp.asarray(spread, bf16),
        spreadt=jnp.asarray(spread.T, bf16),
        place=jnp.asarray(place, bf16),
        placet=jnp.asarray(place.transpose(0, 2, 1), bf16),
        vert=stacked(vert, 2),
        horiz=stacked(horiz, 1),
    )


def stacked(table, axis):
    high = table.astype(bf16)
    low = (table - high.astype(np.float64)).astype(bf16)
    return jnp.asarray(np.concatenate([high, high, low], axis=axis))


def dot(a, b, dims=((1,), (0,))):
    return lax.dot_general(a, b, (dims, ((), ())), preferred_element_type=f32)


def halves(value):
    high = value.astype(bf16)
    low = (value - high.astype(f32)).astype(bf16)
    return high, low


def iota(shape, dim):
    return lax.broadcasted_iota(jnp.int32, shape, dim)


def source_places(ints, table, yc):
    start = jnp.int32(0)
    for o in range(NEAR):
        apart = yc + o - NEAR // 2
        near = jnp.bitwise_and(apart, 7)
        base = CAP * jnp.where(apart == near, near, 8 + jnp.bitwise_and(near, 3))
        for c in range(CAP):
            table[start + c] = base + c
        start = start + ints[CNT + o]
    return [table[ints[LST + e]] for e in range(SLOTS)]


def list_slots(ints, table):
    start = jnp.int32(0)
    for t in range(TILES):
        for c in range(KMAX):
            table[start + c] = jnp.int32(t)
        start = start + ints[TCN + t]
    return [table[e] for e in range(SLOTS)]


def fetch(pairs, sems):
    copies = [pltpu.make_async_copy(src, dst, sems.at[n]) for n, (src, dst) in enumerate(pairs)]
    for copy in copies:
        copy.start()
    return copies


def wait(copies):
    for copy in copies:
        copy.wait()


def pack_kernel(request_in, gauss_in, out, request, gauss, sems):
    wait(fetch([(request_in, request), (gauss_in, gauss)], sems))
    yc = lax.axis_index("yc")
    lane = iota((1, 128), 1) % 32
    for chunk in range(N_YC):
        group = jnp.bitwise_and(yc + NEAR // 2 - chunk, 7)
        ids = []
        for c in range(CAP):
            idx = request[c, 0, group]
            for v in range(VALS):
                out[chunk, 10 * c + v : 10 * c + v + 1, :] = gauss[v, pl.ds(idx, 1), :]
            ids.append(idx)
        row = jnp.where(lane < 10, ids[0], jnp.where(lane < 20, ids[1], ids[2]))
        out[chunk, 30:32, :] = jnp.broadcast_to(row.astype(f32), (2, 128))


def forward_kernel(ints_in, target_in, mom_in, tri_in, spread_in, place_in, own, cross, payload, raws, pair_o,
                   beta_o, ints, group_table, slot_table, target, mom, tri, spread, place, blk, vals, coefs, shades, cols, pair_w, beta, in_sems, sems):
    loads = fetch(
        [
            (ints_in, ints),
            (mom_in, mom), (tri_in, tri), (spread_in, spread), (place_in, place), (target_in, target),
        ],
        in_sems,
    )
    for m in range(12):
        for c in range(CAP):
            src = own[m, 10 * c : 10 * c + 10, :] if m < 8 else cross[m - 8, 10 * c : 10 * c + 10, :]
            blk[m * CAP + c, 0:10, :] = src
    coefs[...] = jnp.zeros_like(coefs)
    cols[...] = jnp.zeros_like(cols)
    wait(loads[:1])
    places = source_places(ints, group_table, lax.axis_index("yc"))
    slots = list_slots(ints, slot_table)
    shades[...] = jnp.zeros_like(shades)
    for e in range(SLOTS):
        raw = blk[places[e]]
        raws[e] = raw
        for v in range(6):
            vals[v, e : e + 1, :] = raw[v : v + 1, :]
        shade = raw[6:10, :]
        high = shade.astype(bf16).astype(f32)
        at = 4 * (e % 2)
        lanes = slice(128 * (e % 2), 128 * (e % 2) + 128)
        shades[e // 2, at : at + 4, lanes] = high
        shades[e // 2, 8 + at : 12 + at, lanes] = shade - high
    mx = vals[0] - 8.0
    my = vals[1] - 8.0
    ca = vals[2]
    cc = vals[4]
    cb = vals[3] * jnp.sqrt(ca * cc)
    logit = vals[5]
    logsig = logit - jnp.log1p(jnp.exp(logit))
    ax = ca * mx + cb * my
    ay = cb * mx + cc * my
    table = [
        log2e * (logsig - 0.5 * (ax * mx + ay * my)),
        log2e * ax,
        log2e * ay,
        (-0.5 * log2e) * ca,
        -log2e * cb,
        (-0.5 * log2e) * cc,
    ]
    for k in range(6):
        high = table[k].astype(bf16).astype(f32)
        rest = table[k] - high
        mid = rest.astype(bf16).astype(f32)
        for e in range(SLOTS):
            lanes = slice(128 * (e % 2), 128 * (e % 2) + 128)
            coefs[e // 2, k : k + 1, lanes] = high[e : e + 1, :]
            coefs[e // 2, 8 + k : 9 + k, lanes] = mid[e : e + 1, :]
            coefs[e // 2, 16 + k : 17 + k, lanes] = (rest - mid)[e : e + 1, :]
    wait(loads[1:])
    upper = iota((8, PIX), 0) < 4
    carry = jnp.zeros((PIX, 128), f32)

    def front(pair):
        first, second = 2 * pair, 2 * pair + 1
        same = slots[first] == slots[second]
        alpha = jnp.exp2(dot(mom[...], coefs[pair].astype(bf16)))
        lost = alpha * (log2e + alpha * (log2e / 2 + alpha * (log2e / 3 + alpha * (log2e / 4))))
        beta[pair] = (alpha * jnp.exp2(lost)).astype(bf16)
        sums = dot(lost.astype(bf16), tri[jnp.where(same, 1, 0)])
        whole = sums[:, 255:256] - lost[:, 255:256]
        return first, second, same, alpha, sums, whole

    ahead = front(0)
    for pair in range(PAIRS):
        first, second, same, alpha, sums, whole = ahead
        if pair + 1 < PAIRS:
            ahead = front(pair + 1)
        whole = jnp.broadcast_to(whole, (PIX, 128))
        if pair:
            carry = jnp.where(slots[first] == slots[first - 1], carry, 0.0)
        later = jnp.where(same, carry, 0.0)
        weight = (jnp.exp2(sums + jnp.concatenate([carry, later], axis=1)) * alpha).astype(bf16)
        carry = whole + later
        pair_w[pair] = weight
        colour = dot(shades[pair].astype(bf16), weight, ((1,), (1,)))
        colour = colour[0:8, :] + colour[8:16, :]
        cols[slots[first]] += jnp.where(upper, colour, 0.0)
        cols[slots[second]] += jnp.where(upper, 0.0, colour)
    copies = (
        pltpu.make_async_copy(pair_w, pair_o, sems.at[0]),
        pltpu.make_async_copy(beta, beta_o, sems.at[1]),
    )
    for copy in copies:
        copy.start()
    row_of = iota((TILE, PIX), 1) // TILE == iota((TILE, PIX), 0)
    lane = iota((TILE, 128), 1)
    pieces = []
    for s in range(TILES):
        colour = cols[s]
        colour = colour[0:4, :] + colour[4:8, :]
        for c in range(CH):
            pieces.append(jnp.where(row_of, jnp.broadcast_to(colour[c : c + 1, :], (TILE, PIX)), 0.0))
    laid = dot(jnp.concatenate(pieces, axis=0).astype(bf16), spread[...])
    tiles = []
    for s in range(TILES):
        tile = jnp.zeros((TILE, 128), f32)
        for c in range(CH):
            at = s * 64 + c * 16
            tile = jnp.where((lane // 16) % 4 == c, laid[at : at + 16, :], tile)
        tiles.append(tile)
    goal = jnp.zeros((SIDE, 128), f32)
    for c in range(CH):
        goal = goal + dot(target[c], place[c])
    body = jnp.concatenate(
        [jnp.where(lane < 64, tiles[0], tiles[1]), jnp.where(lane < 64, tiles[2], tiles[3]), goal], axis=0
    ).astype(bf16)
    row = iota((8, 128), 0)
    tags = jnp.zeros((8, 128), jnp.int32)
    for s in range(TILES):
        tags = jnp.where(row == s, jnp.bitwise_and(ints[REN + s], 3), tags)
    tags = tags.astype(f32).astype(bf16)
    for q in range(N_IMG * N_ZQ):
        payload[q, 0:64, :] = body
        payload[q, 64:72, :] = tags
    for copy in copies:
        copy.wait()


def error_kernel(got, vert, placet, up, edge, err_own, rendered, errs, images):
    lane = iota((TILE, 128), 1)
    half = lane // 64
    halff = half.astype(f32)
    for strip in range(N_IMG):
        for home in range(N_ZQ):
            acc = [jnp.zeros((TILE, 128), f32), jnp.zeros((TILE, 128), f32)]
            for s in range(TILES):
                src = strip * 4 + (home - s) % 4
                both = got[src, 16 * (s // 2) : 16 * (s // 2) + 16, :].astype(f32)
                turned = pltpu.roll(both, 64, 1)
                tile = jnp.where(half == s % 2, both, turned)
                tag = jnp.broadcast_to(got[src, 64:72, :].astype(f32)[s : s + 1, :], (TILE, 128)) - halff
                acc[0] = jnp.where(tag == 0.0, tile, acc[0])
                acc[1] = jnp.where(tag == 2.0, tile, acc[1])
            image = jnp.concatenate(acc, axis=0)
            images[strip * 4 + home] = image
            goal = got[strip * 4 + home, 32:64, :].astype(f32)
            errs[strip * 32 : strip * 32 + 32, home * 128 : home * 128 + 128] = image - goal
    img = lax.axis_index("img")
    high, low = halves(errs[...])
    blurred = dot(vert[img], jnp.concatenate([high, low, high], axis=0))
    for home in range(N_ZQ):
        up[home] = blurred[:, home * 128 : home * 128 + 128]
        edge[home] = blurred[:, home * 128 : home * 128 + 128].astype(bf16)
        err_own[home] = errs[pl.ds(pl.multiple_of(img * 32, 32), 32), home * 128 : home * 128 + 128]
    mine = images[img * 4 + lax.axis_index("zq")].astype(bf16)
    for c in range(CH):
        rendered[c] = dot(mine, placet[c]).astype(bf16)


def backward_kernel(ints_in, horiz_in, placet_in, spreadt_in, momt_in, trib_in,
                    pair_o, beta_o, up, got_mate, got_other, err_own, raws, own, cross,
                    grad_out, msg_own, msg_cross,
                    ints, group_table, slot_table, horiz, placet, spreadt, momt, trib, pair_w, beta,
                    ext, back, grads, vals, sums, blk, pack, shades, shade_sums, sems):
    loads = fetch(
        [
            (ints_in, ints),
            (horiz_in, horiz), (placet_in, placet), (spreadt_in, spreadt), (momt_in, momt), (trib_in, trib),
            (pair_o, pair_w), (beta_o, beta),
        ],
        sems,
    )
    yc = lax.axis_index("yc")
    zq = lax.axis_index("zq")
    parity = jnp.bitwise_and(yc, 1)
    place_mid = lax.axis_index("zr") * N_YC + yc
    lane32 = iota((SIDE, 128), 1)
    for home in range(N_ZQ):
        at_left = home - jnp.where(place_mid == 0, 1, 0)
        at_right = home + jnp.where(place_mid == 31, 1, 0)
        in_left = at_left >= 0
        in_right = at_right < N_ZQ
        at_left = jnp.maximum(at_left, 0)
        at_right = jnp.minimum(at_right, N_ZQ - 1)
        left = jnp.where(parity == 0, got_other[at_left], got_mate[at_left])
        right = jnp.where(parity == 0, got_mate[at_right], got_other[at_right])
        left = jnp.where(in_left, left.astype(f32), 0.0)
        right = jnp.where(in_right, right.astype(f32), 0.0)
        rows = slice(home * 32, home * 32 + 32)
        ext[rows, 0:128] = up[home]
        ext[rows, 128:256] = jnp.where(lane32 < 64, right, left)
    wait(loads[:4])
    high, low = halves(ext[...])
    split = jnp.concatenate([high, low, high], axis=1)
    back[...] = dot(split, horiz[0])

    @pl.when(place_mid == 0)
    def _():
        back[0:32, :] = dot(split[0:32, :], horiz[1])

    @pl.when(place_mid == 31)
    def _():
        back[96:128, :] = dot(split[96:128, :], horiz[2])

    for home in range(N_ZQ):
        total = loss_weight * (
            (1.0 - lam_weight) * err_own[home] + lam_weight * back[home * 32 : home * 32 + 32, :]
        )
        grads[home] = total.astype(bf16).astype(f32)
    mine = grads[zq].astype(bf16)
    for c in range(CH):
        grad_out[c] = dot(mine, placet[c]).astype(bf16)

    lane = iota((TILE, 128), 1)
    pieces = []
    for s in range(TILES):
        home = jnp.bitwise_and(zq + s, 3)
        local = jnp.bitwise_and(ints[REN + s], 3)
        down = local // 2
        across = jnp.bitwise_and(local, 1)
        tile = grads[home, pl.ds(pl.multiple_of(down * 16, 16), 16), :]
        for c in range(CH):
            pieces.append(jnp.where(lane // 16 == across * 4 + c, tile, 0.0))
    laid = dot(jnp.concatenate(pieces, axis=0).astype(bf16), spreadt[...])
    row_of = iota((TILE, PIX), 1) // TILE == iota((TILE, PIX), 0)
    lines = []
    for s in range(TILES):
        four = []
        for c in range(CH):
            at = s * 64 + c * 16
            four.append(jnp.sum(jnp.where(row_of, laid[at : at + 16, :], 0.0), axis=0, keepdims=True))
        lines = lines + four + four
    grad_rows = jnp.concatenate(lines, axis=0)
    grad_cols = jnp.transpose(grad_rows).astype(bf16)
    grad_rows = grad_rows.astype(bf16)

    slots = list_slots(ints, slot_table)
    places = source_places(ints, group_table, yc)
    shades[...] = jnp.zeros_like(shades)
    for e in range(SLOTS):
        shade = raws[e, 6:10, :]
        high = shade.astype(bf16).astype(f32)
        at = pl.ds(pl.multiple_of(slots[e] * 8, 8), 8)
        shades[e // 2, at, 128 * (e % 2) : 128 * (e % 2) + 128] = jnp.concatenate([high, shade - high], axis=0)
        for k in range(6):
            vals[k, e : e + 1, :] = raws[e, k : k + 1, :]
    wait(loads[4:])
    carry = jnp.zeros((PIX, 128), f32)

    def front(pair):
        first, second = 2 * pair, 2 * pair + 1
        same = slots[first] == slots[second]
        product = pair_w[pair].astype(f32) * dot(grad_cols, shades[pair].astype(bf16))
        after = dot(product.astype(bf16), trib[jnp.where(same, 1, 0)])
        return first, second, same, product, after, after[:, 0:1] + product[:, 0:1]

    ahead = front(PAIRS - 1)
    for pair in reversed(range(PAIRS)):
        first, second, same, product, after, whole = ahead
        if pair:
            ahead = front(pair - 1)
        whole = jnp.broadcast_to(whole, (PIX, 128))
        if pair < PAIRS - 1:
            carry = jnp.where(slots[second] == slots[second + 1], carry, 0.0)
        earlier = jnp.where(same, carry, 0.0)
        unit = product - (after + jnp.concatenate([earlier, carry], axis=1)) * beta[pair].astype(f32)
        carry = whole + earlier
        high, low = halves(unit)
        moment = dot(momt[...], high) + dot(momt[...], low)
        shade_grad = dot(grad_rows, pair_w[pair])
        for s in range(TILES):
            shade_sums[pair, s] = shade_grad[8 * s : 8 * s + 8, :]
        for k in range(6):
            sums[k, first : first + 1, :] = moment[k : k + 1, :128]
            sums[k, second : second + 1, :] = moment[k : k + 1, 128:]
    for e in range(SLOTS):
        shade_grad = shade_sums[e // 2, slots[e]]
        for c in range(CH):
            sums[6 + c, e : e + 1, :] = shade_grad[c : c + 1, 128 * (e % 2) : 128 * (e % 2) + 128]
    mx = vals[0] - 8.0
    my = vals[1] - 8.0
    ca = vals[2]
    rho = vals[3]
    cc = vals[4]
    opaque = jax.nn.sigmoid(vals[5])
    m0 = -0.5 * sums[0]
    m1 = -0.5 * sums[1]
    m2 = -0.5 * sums[2]
    m3 = -0.5 * sums[3]
    m4 = -0.5 * sums[4]
    m5 = -0.5 * sums[5]
    along_x = m1 - mx * m0
    along_y = m2 - my * m0
    square_x = m3 - 2.0 * mx * m1 + mx * mx * m0
    square_y = m5 - 2.0 * my * m2 + my * my * m0
    mixed = m4 - mx * m2 - my * m1 + mx * my * m0
    root = jnp.sqrt(ca * cc)
    cb = rho * root
    out = [
        -2.0 * (ca * along_x + cb * along_y),
        -2.0 * (cb * along_x + cc * along_y),
        square_x + rho * jnp.sqrt(cc / ca) * mixed,
        2.0 * root * mixed,
        square_y + rho * jnp.sqrt(ca / cc) * mixed,
        (1.0 - opaque) * sums[0],
    ] + [sums[6 + c] for c in range(CH)]
    blk[...] = jnp.zeros_like(blk)
    for e in range(SLOTS):
        for v in range(VALS):
            blk[places[e], v : v + 1, :] = out[v][e : e + 1, :]
    lane1 = iota((2, 128), 1)
    group = jnp.where(lane1 // 32 == jnp.bitwise_and(yc, 3), 1.0, 0.0)
    for m in range(12):
        for c in range(CAP):
            pack[m, 10 * c : 10 * c + 10, :] = blk[m * CAP + c, 0:10, :]
        ids = own[m, 30:32, :] if m < 8 else cross[m - 8, 30:32, :]
        pack[m, 30:32, :] = ids * group
    msg_own[...] = pack[0:8].astype(bf16)
    msg_cross[...] = pack[8:12].astype(bf16)


def collect_kernel(got, out):
    lane = iota((1, 128), 1)
    line = lane % 32
    value = jnp.where(line < 10, line, jnp.where(line < 20, line - 10, line - 20))
    goals = []
    for quad in range(8):
        ids = jnp.zeros((1, 128), f32)
        for m in range(4):
            ids = ids + got[quad * 4 + m, 16:32, :].astype(f32)[14:15, :]
        goals.append(jnp.where(line < 30, ids.astype(jnp.int32) + value * BLK_DEV, -1))
    flat = got[...].reshape(32 * MSG, 128)
    rows = 2 * BLK_DEV
    for part in range(VALS // 2):
        here = iota((rows, 128), 0) + part * rows
        hits = [jnp.where(here == goal, 1.0, 0.0).astype(bf16) for goal in goals]
        total = dot(jnp.concatenate(hits, axis=1), flat)
        out[2 * part] = total[:BLK_DEV]
        out[2 * part + 1] = total[BLK_DEV:]


VM = pl.BlockSpec(memory_space=pltpu.VMEM)
SM = pl.BlockSpec(memory_space=pltpu.SMEM)
HB = pl.BlockSpec(memory_space=pltpu.HBM)


def call(kernel, ins, outs, scratch, name, limit=16):
    return pl.pallas_call(
        kernel,
        out_shape=tuple(jax.ShapeDtypeStruct(shape, dtype) for shape, dtype, _ in outs),
        in_specs=ins,
        out_specs=tuple(space for _, _, space in outs),
        scratch_shapes=scratch,
        compiler_params=pltpu.CompilerParams(vmem_limit_bytes=limit << 20 if limit else None),
        name=name,
    )


def on_device(gaussians, target, request, near_counts, render_tile, tile_lists, tile_counts):
    table = constants()
    yc = lax.axis_index("yc")
    wanted = request.transpose(0, 3, 1, 2).reshape(CAP, 1, NEAR)
    n_gs = N_ZQ * N_ZR * N_YC
    up_route = []
    for r in range(n_gs):
        j = r % N_YC
        if j < 4:
            up_route.append((r, (r + N_YC) % n_gs))
        elif j > 4:
            up_route.append((r, (r - N_YC) % n_gs))
    back_route = [(b, a) for a, b in up_route]
    group = N_IMG * N_ZQ
    vm = pltpu.VMEM

    small = [pltpu.SMEM((32,), jnp.int32) for _ in range(3)]
    dma = pltpu.SemaphoreType.DMA

    (sent,) = call(
        pack_kernel,
        [HB, HB],
        [((N_YC, MSG, 128), f32, VM)],
        [pltpu.SMEM((CAP, 1, NEAR), jnp.int32), vm((VALS, BLK_DEV, 128), f32), dma((2,))],
        "pack",
        None,
    )(wanted, gaussians.transpose(1, 0, 2))
    own = lax.all_to_all(sent, "yc", 0, 0, tiled=True)
    own, near_counts, tile_lists, tile_counts, render_tile = lax.optimization_barrier(
        (own, near_counts, tile_lists, tile_counts, render_tile)
    )
    ints = jnp.concatenate(
        [near_counts.reshape(NEAR), tile_lists.reshape(SLOTS), tile_counts.reshape(TILES), render_tile.reshape(TILES)]
    )
    crossing = jnp.where(yc < 4, own[4:8], own[0:4])
    cross = lax.ppermute(crossing, GS, up_route)

    payload, raws, pair_w, beta = call(
        forward_kernel,
        [HB] * 6 + [VM] * 2,
        [
            ((group, 72, 128), bf16, VM),
            ((SLOTS, 16, 128), f32, VM),
            ((PAIRS, PIX, 256), bf16, HB),
            ((PAIRS, PIX, 256), bf16, HB),
        ],
        small
        + [
            vm((CH, SIDE, SIDE), bf16),
            vm((PIX, 32), bf16),
            vm((2, 256, 256), bf16),
            vm((PIX, 128), bf16),
            vm((CH, SIDE, 128), bf16),
            vm((36, 16, 128), f32),
            vm((6, 16, 128), f32),
            vm((PAIRS, 32, 256), f32),
            vm((PAIRS, 16, 256), f32),
            vm((TILES, 8, PIX), f32),
            vm((PAIRS, PIX, 256), bf16),
            vm((PAIRS, PIX, 256), bf16),
            dma((6,)),
            dma((2,)),
        ],
        "forward",
    )(
        ints, target, table["mom"], table["tri"], table["spread"], table["place"],
        own, cross,
    )
    got = lax.all_to_all(payload, ("img", "zq"), 0, 0, tiled=True)

    up, edge, err_own, rendered = call(
        error_kernel,
        [VM] * 3,
        [
            ((N_ZQ, SIDE, 128), f32, VM),
            ((N_ZQ, SIDE, 128), bf16, VM),
            ((N_ZQ, SIDE, 128), f32, VM),
            ((CH, SIDE, SIDE), bf16, VM),
        ],
        [vm((N_IMG * SIDE, 512), f32), vm((16, SIDE, 128), f32)],
        "error",
    )(got, table["vert"], table["placet"])

    other = [((2 * c - 1) % n_gs, 2 * c) for c in range(n_gs // 2)]
    other = other + [(b, a) for a, b in other]
    got_other = lax.ppermute(edge, GS, other)
    got_mate = lax.ppermute(edge, GS, [(r, r ^ 1) for r in range(n_gs)])

    pixel_grad, msg_own, msg_cross = call(
        backward_kernel,
        [HB] * 8 + [VM] * 7,
        [((CH, SIDE, SIDE), bf16, VM), ((N_YC, MSG, 128), bf16, VM), ((4, MSG, 128), bf16, VM)],
        small
        + [
            vm((3, 768, 128), bf16),
            vm((CH, 128, SIDE), bf16),
            vm((128, PIX), bf16),
            vm((16, PIX), bf16),
            vm((2, 256, 256), bf16),
            vm((PAIRS, PIX, 256), bf16),
            vm((PAIRS, PIX, 256), bf16),
            vm((128, 256), f32),
            vm((128, 128), f32),
            vm((N_ZQ, SIDE, 128), f32),
            vm((6, 16, 128), f32),
            vm((10, 16, 128), f32),
            vm((36, 16, 128), f32),
            vm((12, MSG, 128), f32),
            vm((PAIRS, 32, 256), f32),
            vm((PAIRS, TILES, 8, 256), f32),
            dma((8,)),
        ],
        "backward",
    )(
        ints, table["horiz"], table["placet"], table["spreadt"], table["momt"],
        table["trib"], pair_w, beta, up, got_mate, got_other, err_own, raws, own, cross,
    )
    returned = lax.ppermute(msg_cross, GS, back_route)
    apart = jnp.arange(N_YC) + NEAR // 2 - yc
    straight = ((apart >= 0) & (apart < NEAR))[:, None, None]
    merged = jnp.where(straight, msg_own, jnp.concatenate([returned, returned], axis=0))
    spread_out = jnp.broadcast_to(merged[None], (N_IMG, N_YC, MSG, 128)).reshape(N_IMG * N_YC, MSG, 128)
    all_msgs = lax.all_to_all(spread_out, ("img", "yc"), 0, 0, tiled=True)
    (summed,) = call(collect_kernel, [VM], [((VALS, BLK_DEV, 128), f32, VM)], [], "collect")(all_msgs)
    return (rendered, pixel_grad, summed.transpose(1, 0, 2))


def solution(mesh):
    wide = Mesh(mesh.devices.reshape(N_IMG, N_ZQ, N_ZR, N_YC), ("img", "zq", "zr", "yc"))
    in_specs = (
        P(GS, None, None),
        P(None, "img", GS),
        P("img", GS, None, None),
        P("img", GS, None),
        P("img", GS, None),
        P("img", GS, None),
        P("img", GS, None),
    )
    out_specs = (P(None, "img", GS), P(None, "img", GS), P(GS, None, None))
    return jax.shard_map(on_device, mesh=wide, in_specs=in_specs, out_specs=out_specs, check_vma=False)
```

```python
import functools
import math

import jax
import jax.numpy as jnp
import numpy as np
from jax import lax
from jax.experimental import pallas as pl
from jax.experimental.pallas import tpu as pltpu
from jax.sharding import Mesh
from jax.sharding import PartitionSpec as P

TILE = 16
BLOCK = 128
CH = 4
SLOTS = 16
PAIRS = SLOTS // 2
NEAR = 8
CAP = 3
RADIUS = 5
KMAX = 6
TILES = 4
PIX = 256
N_IMG = 4
N_ZQ = 4
N_ZR = 4
N_YC = 8
BLK_DEV = 96
VALS = 10
MSG = 32
SIDE = 32

lam_weight = 0.2
loss_weight = 16.0
sigma_window = 1.5
log2e = math.log2(math.e)

f32 = jnp.float32
bf16 = jnp.bfloat16
GS = ("zq", "zr", "yc")

CNT, LST, TCN, REN = 0, 8, 24, 28


def constants():
    lane = np.arange(128)
    pix = np.arange(PIX)
    x = pix % TILE - 7.5
    y = pix // TILE - 7.5
    moments = np.stack([np.ones(PIX), x, y, x * x, x * y, y * y], axis=1)
    mom = np.zeros((PIX, 32))
    for part in range(3):
        mom[:, part * 8 : part * 8 + 6] = moments
    momt = np.zeros((16, PIX))
    momt[:6] = moments.T
    long = (np.arange(256)[:, None] < np.arange(256)[None, :]).astype(float)
    alone = long * (np.arange(256)[:, None] // 128 == np.arange(256)[None, :] // 128)
    tri = -np.stack([alone, long])
    trib = np.stack([alone.T, long.T])
    spread = (pix[:, None] % 16 == lane[None, :] % 16).astype(float)
    place = np.zeros((CH, SIDE, 128))
    for c in range(CH):
        for col in range(SIDE):
            place[c, col, (col // 16) * 64 + c * 16 + col % 16] = 1.0
    offsets = np.arange(-RADIUS, RADIUS + 1)
    window = np.exp(-offsets * offsets / (2.0 * sigma_window**2))
    window = window / window.sum()
    rows = N_IMG * SIDE

    def band(count):
        full = np.zeros((count, count))
        for a in range(count):
            for b in range(max(0, a - RADIUS), min(count, a + RADIUS + 1)):
                full[a, b] = window[b - a + RADIUS]
        return full

    vert = band(rows)
    vert = (vert @ vert).reshape(N_IMG, SIDE, rows)
    wide = band(96)
    inner = (wide @ wide)[16:80, 32:64]
    edge = band(64)
    edge = edge @ edge
    left = np.zeros((64, 32))
    left[16:] = edge[:48, :32]
    right = np.zeros((64, 32))
    right[:48] = edge[16:, 32:]
    horiz = np.zeros((3, 256, 128))
    for kind, table in enumerate((inner, left, right)):
        for src in range(64):
            strip = src // 16 - 1
            for c in range(CH):
                if 0 <= strip < 2:
                    row = strip * 64 + c * 16 + src % 16
                elif strip == 2:
                    row = 128 + c * 16 + src % 16
                else:
                    row = 192 + c * 16 + src % 16
                for dst in range(32):
                    horiz[kind, row, (dst // 16) * 64 + c * 16 + dst % 16] = table[src, dst]
    return dict(
        mom=jnp.asarray(mom, bf16),
        momt=jnp.asarray(momt, bf16),
        tri=jnp.asarray(tri, bf16),
        trib=jnp.asarray(trib, bf16),
        spread=jnp.asarray(spread, bf16),
        spreadt=jnp.asarray(spread.T, bf16),
        place=jnp.asarray(place, bf16),
        placet=jnp.asarray(place.transpose(0, 2, 1), bf16),
        vert=stacked(vert, 2),
        horiz=stacked(horiz, 1),
    )


def stacked(table, axis):
    high = table.astype(bf16)
    low = (table - high.astype(np.float64)).astype(bf16)
    return jnp.asarray(np.concatenate([high, high, low], axis=axis))


def dot(a, b, dims=((1,), (0,))):
    return lax.dot_general(a, b, (dims, ((), ())), preferred_element_type=f32)


def halves(value):
    high = value.astype(bf16)
    low = (value - high.astype(f32)).astype(bf16)
    return high, low


def iota(shape, dim):
    return lax.broadcasted_iota(jnp.int32, shape, dim)


def source_places(ints, table, yc):
    start = jnp.int32(0)
    for o in range(NEAR):
        apart = yc + o - NEAR // 2
        near = jnp.bitwise_and(apart, 7)
        base = CAP * jnp.where(apart == near, near, 8 + jnp.bitwise_and(near, 3))
        for c in range(CAP):
            table[start + c] = base + c
        start = start + ints[CNT + o]
    return [table[ints[LST + e]] for e in range(SLOTS)]


def list_slots(ints, table):
    start = jnp.int32(0)
    for t in range(TILES):
        for c in range(KMAX):
            table[start + c] = jnp.int32(t)
        start = start + ints[TCN + t]
    return [table[e] for e in range(SLOTS)]


def fetch(pairs, sems):
    copies = [pltpu.make_async_copy(src, dst, sems.at[n]) for n, (src, dst) in enumerate(pairs)]
    for copy in copies:
        copy.start()
    return copies


def wait(copies):
    for copy in copies:
        copy.wait()


def pack_kernel(request_in, gauss_in, out, request, gauss, sems):
    wait(fetch([(request_in, request), (gauss_in, gauss)], sems))
    yc = lax.axis_index("yc")
    lane = iota((1, 128), 1) % 32
    for chunk in range(N_YC):
        group = jnp.bitwise_and(yc + NEAR // 2 - chunk, 7)
        ids = []
        for c in range(CAP):
            idx = request[c, 0, group]
            for v in range(VALS):
                out[chunk, 10 * c + v : 10 * c + v + 1, :] = gauss[v, pl.ds(idx, 1), :]
            ids.append(idx)
        row = jnp.where(lane < 10, ids[0], jnp.where(lane < 20, ids[1], ids[2]))
        out[chunk, 30:32, :] = jnp.broadcast_to(row.astype(f32), (2, 128))


def forward_kernel(ints_in, target_in, mom_in, tri_in, spread_in, place_in, own, cross, payload, raws, pair_w,
                   beta, ints, group_table, slot_table, target, mom, tri, spread, place, blk, vals, coefs, shades, cols, in_sems):
    loads = fetch(
        [
            (ints_in, ints),
            (mom_in, mom), (tri_in, tri), (spread_in, spread), (place_in, place), (target_in, target),
        ],
        in_sems,
    )
    for m in range(12):
        for c in range(CAP):
            src = own[m, 10 * c : 10 * c + 10, :] if m < 8 else cross[m - 8, 10 * c : 10 * c + 10, :]
            blk[m * CAP + c, 0:10, :] = src
    coefs[...] = jnp.zeros_like(coefs)
    cols[...] = jnp.zeros_like(cols)
    wait(loads[:1])
    places = source_places(ints, group_table, lax.axis_index("yc"))
    slots = list_slots(ints, slot_table)
    shades[...] = jnp.zeros_like(shades)
    for e in range(SLOTS):
        raw = blk[places[e]]
        raws[e] = raw
        for v in range(6):
            vals[v, e : e + 1, :] = raw[v : v + 1, :]
        shade = raw[6:10, :]
        high = shade.astype(bf16).astype(f32)
        at = 4 * (e % 2)
        lanes = slice(128 * (e % 2), 128 * (e % 2) + 128)
        shades[e // 2, at : at + 4, lanes] = high
        shades[e // 2, 8 + at : 12 + at, lanes] = shade - high
    mx = vals[0] - 8.0
    my = vals[1] - 8.0
    ca = vals[2]
    cc = vals[4]
    cb = vals[3] * jnp.sqrt(ca * cc)
    logit = vals[5]
    logsig = logit - jnp.log1p(jnp.exp(logit))
    ax = ca * mx + cb * my
    ay = cb * mx + cc * my
    table = [
        log2e * (logsig - 0.5 * (ax * mx + ay * my)),
        log2e * ax,
        log2e * ay,
        (-0.5 * log2e) * ca,
        -log2e * cb,
        (-0.5 * log2e) * cc,
    ]
    for k in range(6):
        high = table[k].astype(bf16).astype(f32)
        rest = table[k] - high
        mid = rest.astype(bf16).astype(f32)
        for e in range(SLOTS):
            lanes = slice(128 * (e % 2), 128 * (e % 2) + 128)
            coefs[e // 2, k : k + 1, lanes] = high[e : e + 1, :]
            coefs[e // 2, 8 + k : 9 + k, lanes] = mid[e : e + 1, :]
            coefs[e // 2, 16 + k : 17 + k, lanes] = (rest - mid)[e : e + 1, :]
    wait(loads[1:])
    upper = iota((8, PIX), 0) < 4
    carry = jnp.zeros((PIX, 128), f32)

    def front(pair):
        first, second = 2 * pair, 2 * pair + 1
        same = slots[first] == slots[second]
        alpha = jnp.exp2(dot(mom[...], coefs[pair].astype(bf16)))
        lost = alpha * (log2e + alpha * (log2e / 2 + alpha * (log2e / 3 + alpha * (log2e / 4))))
        beta[pair] = (alpha * jnp.exp2(lost)).astype(bf16)
        high, low = halves(lost)
        earlier = tri[jnp.where(same, 1, 0)]
        sums = dot(high, earlier) + dot(low, earlier)
        whole = sums[:, 255:256] - lost[:, 255:256]
        return first, second, same, alpha, sums, whole

    ahead = front(0)
    for pair in range(PAIRS):
        first, second, same, alpha, sums, whole = ahead
        if pair + 1 < PAIRS:
            ahead = front(pair + 1)
        whole = jnp.broadcast_to(whole, (PIX, 128))
        if pair:
            carry = jnp.where(slots[first] == slots[first - 1], carry, 0.0)
        later = jnp.where(same, carry, 0.0)
        high, low = halves(jnp.exp2(sums + jnp.concatenate([carry, later], axis=1)) * alpha)
        pair_w[pair] = high
        carry = whole + later
        shade = shades[pair].astype(bf16)
        colour = dot(shade, high, ((1,), (1,))) + dot(shade, low, ((1,), (1,)))
        colour = colour[0:8, :] + colour[8:16, :]
        cols[slots[first]] += jnp.where(upper, colour, 0.0)
        cols[slots[second]] += jnp.where(upper, 0.0, colour)
    row_of = iota((TILE, PIX), 1) // TILE == iota((TILE, PIX), 0)
    lane = iota((TILE, 128), 1)
    pieces = []
    for s in range(TILES):
        colour = cols[s]
        colour = colour[0:4, :] + colour[4:8, :]
        for c in range(CH):
            pieces.append(jnp.where(row_of, jnp.broadcast_to(colour[c : c + 1, :], (TILE, PIX)), 0.0))
    laid = dot(jnp.concatenate(pieces, axis=0).astype(bf16), spread[...])
    tiles = []
    for s in range(TILES):
        tile = jnp.zeros((TILE, 128), f32)
        for c in range(CH):
            at = s * 64 + c * 16
            tile = jnp.where((lane // 16) % 4 == c, laid[at : at + 16, :], tile)
        tiles.append(tile)
    goal = jnp.zeros((SIDE, 128), f32)
    for c in range(CH):
        goal = goal + dot(target[c], place[c])
    body = jnp.concatenate(
        [jnp.where(lane < 64, tiles[0], tiles[1]), jnp.where(lane < 64, tiles[2], tiles[3]), goal], axis=0
    ).astype(bf16)
    row = iota((8, 128), 0)
    tags = jnp.zeros((8, 128), jnp.int32)
    for s in range(TILES):
        tags = jnp.where(row == s, jnp.bitwise_and(ints[REN + s], 3), tags)
    tags = tags.astype(f32).astype(bf16)
    for q in range(N_IMG * N_ZQ):
        payload[q, 0:64, :] = body
        payload[q, 64:72, :] = tags


def error_kernel(got, vert, placet, up, edge, err_own, rendered, errs, images):
    lane = iota((TILE, 128), 1)
    half = lane // 64
    halff = half.astype(f32)
    for strip in range(N_IMG):
        for home in range(N_ZQ):
            acc = [jnp.zeros((TILE, 128), f32), jnp.zeros((TILE, 128), f32)]
            for s in range(TILES):
                src = strip * 4 + (home - s) % 4
                both = got[src, 16 * (s // 2) : 16 * (s // 2) + 16, :].astype(f32)
                turned = pltpu.roll(both, 64, 1)
                tile = jnp.where(half == s % 2, both, turned)
                tag = jnp.broadcast_to(got[src, 64:72, :].astype(f32)[s : s + 1, :], (TILE, 128)) - halff
                acc[0] = jnp.where(tag == 0.0, tile, acc[0])
                acc[1] = jnp.where(tag == 2.0, tile, acc[1])
            image = jnp.concatenate(acc, axis=0)
            images[strip * 4 + home] = image
            goal = got[strip * 4 + home, 32:64, :].astype(f32)
            errs[strip * 32 : strip * 32 + 32, home * 128 : home * 128 + 128] = image - goal
    img = lax.axis_index("img")
    high, low = halves(errs[...])
    blurred = dot(vert[img], jnp.concatenate([high, low, high], axis=0))
    for home in range(N_ZQ):
        up[home] = blurred[:, home * 128 : home * 128 + 128]
        edge[home] = blurred[:, home * 128 : home * 128 + 128].astype(bf16)
        err_own[home] = errs[pl.ds(pl.multiple_of(img * 32, 32), 32), home * 128 : home * 128 + 128]
    mine = images[img * 4 + lax.axis_index("zq")].astype(bf16)
    for c in range(CH):
        rendered[c] = dot(mine, placet[c]).astype(bf16)


def backward_kernel(ints_in, horiz_in, placet_in, spreadt_in, momt_in, trib_in,
                    up, got_mate, got_other, err_own, raws, pair_w, beta, own, cross,
                    grad_out, msg_own, msg_cross,
                    ints, group_table, slot_table, horiz, placet, spreadt, momt, trib,
                    ext, back, grads, vals, sums, blk, pack, shades, shade_sums, sems):
    loads = fetch(
        [
            (ints_in, ints),
            (horiz_in, horiz), (placet_in, placet), (spreadt_in, spreadt), (momt_in, momt), (trib_in, trib),
        ],
        sems,
    )
    yc = lax.axis_index("yc")
    zq = lax.axis_index("zq")
    parity = jnp.bitwise_and(yc, 1)
    place_mid = lax.axis_index("zr") * N_YC + yc
    lane32 = iota((SIDE, 128), 1)
    for home in range(N_ZQ):
        at_left = home - jnp.where(place_mid == 0, 1, 0)
        at_right = home + jnp.where(place_mid == 31, 1, 0)
        in_left = at_left >= 0
        in_right = at_right < N_ZQ
        at_left = jnp.maximum(at_left, 0)
        at_right = jnp.minimum(at_right, N_ZQ - 1)
        left = jnp.where(parity == 0, got_other[at_left], got_mate[at_left])
        right = jnp.where(parity == 0, got_mate[at_right], got_other[at_right])
        left = jnp.where(in_left, left.astype(f32), 0.0)
        right = jnp.where(in_right, right.astype(f32), 0.0)
        rows = slice(home * 32, home * 32 + 32)
        ext[rows, 0:128] = up[home]
        ext[rows, 128:256] = jnp.where(lane32 < 64, right, left)
    wait(loads[:4])
    high, low = halves(ext[...])
    split = jnp.concatenate([high, low, high], axis=1)
    back[...] = dot(split, horiz[0])

    @pl.when(place_mid == 0)
    def _():
        back[0:32, :] = dot(split[0:32, :], horiz[1])

    @pl.when(place_mid == 31)
    def _():
        back[96:128, :] = dot(split[96:128, :], horiz[2])

    for home in range(N_ZQ):
        total = loss_weight * (
            (1.0 - lam_weight) * err_own[home] + lam_weight * back[home * 32 : home * 32 + 32, :]
        )
        grads[home] = total.astype(bf16).astype(f32)
    mine = grads[zq].astype(bf16)
    for c in range(CH):
        grad_out[c] = dot(mine, placet[c]).astype(bf16)

    lane = iota((TILE, 128), 1)
    pieces = []
    for s in range(TILES):
        home = jnp.bitwise_and(zq + s, 3)
        local = jnp.bitwise_and(ints[REN + s], 3)
        down = local // 2
        across = jnp.bitwise_and(local, 1)
        tile = grads[home, pl.ds(pl.multiple_of(down * 16, 16), 16), :]
        for c in range(CH):
            pieces.append(jnp.where(lane // 16 == across * 4 + c, tile, 0.0))
    laid = dot(jnp.concatenate(pieces, axis=0).astype(bf16), spreadt[...])
    row_of = iota((TILE, PIX), 1) // TILE == iota((TILE, PIX), 0)
    lines = []
    for s in range(TILES):
        four = []
        for c in range(CH):
            at = s * 64 + c * 16
            four.append(jnp.sum(jnp.where(row_of, laid[at : at + 16, :], 0.0), axis=0, keepdims=True))
        lines = lines + four + four
    grad_rows = jnp.concatenate(lines, axis=0)
    grad_cols = jnp.transpose(grad_rows).astype(bf16)
    grad_rows = grad_rows.astype(bf16)

    slots = list_slots(ints, slot_table)
    places = source_places(ints, group_table, yc)
    shades[...] = jnp.zeros_like(shades)
    for e in range(SLOTS):
        shade = raws[e, 6:10, :]
        high = shade.astype(bf16).astype(f32)
        at = pl.ds(pl.multiple_of(slots[e] * 8, 8), 8)
        shades[e // 2, at, 128 * (e % 2) : 128 * (e % 2) + 128] = jnp.concatenate([high, shade - high], axis=0)
        for k in range(6):
            vals[k, e : e + 1, :] = raws[e, k : k + 1, :]
    wait(loads[4:])
    carry = jnp.zeros((PIX, 128), f32)

    def front(pair):
        first, second = 2 * pair, 2 * pair + 1
        same = slots[first] == slots[second]
        product = pair_w[pair].astype(f32) * dot(grad_cols, shades[pair].astype(bf16))
        after = dot(product.astype(bf16), trib[jnp.where(same, 1, 0)])
        return first, second, same, product, after, after[:, 0:1] + product[:, 0:1]

    ahead = front(PAIRS - 1)
    for pair in reversed(range(PAIRS)):
        first, second, same, product, after, whole = ahead
        if pair:
            ahead = front(pair - 1)
        whole = jnp.broadcast_to(whole, (PIX, 128))
        if pair < PAIRS - 1:
            carry = jnp.where(slots[second] == slots[second + 1], carry, 0.0)
        earlier = jnp.where(same, carry, 0.0)
        unit = product - (after + jnp.concatenate([earlier, carry], axis=1)) * beta[pair].astype(f32)
        carry = whole + earlier
        high, low = halves(unit)
        moment = dot(momt[...], high) + dot(momt[...], low)
        shade_grad = dot(grad_rows, pair_w[pair])
        for s in range(TILES):
            shade_sums[pair, s] = shade_grad[8 * s : 8 * s + 8, :]
        for k in range(6):
            sums[k, first : first + 1, :] = moment[k : k + 1, :128]
            sums[k, second : second + 1, :] = moment[k : k + 1, 128:]
    for e in range(SLOTS):
        shade_grad = shade_sums[e // 2, slots[e]]
        for c in range(CH):
            sums[6 + c, e : e + 1, :] = shade_grad[c : c + 1, 128 * (e % 2) : 128 * (e % 2) + 128]
    mx = vals[0] - 8.0
    my = vals[1] - 8.0
    ca = vals[2]
    rho = vals[3]
    cc = vals[4]
    opaque = jax.nn.sigmoid(vals[5])
    m0 = -0.5 * sums[0]
    m1 = -0.5 * sums[1]
    m2 = -0.5 * sums[2]
    m3 = -0.5 * sums[3]
    m4 = -0.5 * sums[4]
    m5 = -0.5 * sums[5]
    along_x = m1 - mx * m0
    along_y = m2 - my * m0
    square_x = m3 - 2.0 * mx * m1 + mx * mx * m0
    square_y = m5 - 2.0 * my * m2 + my * my * m0
    mixed = m4 - mx * m2 - my * m1 + mx * my * m0
    root = jnp.sqrt(ca * cc)
    cb = rho * root
    out = [
        -2.0 * (ca * along_x + cb * along_y),
        -2.0 * (cb * along_x + cc * along_y),
        square_x + rho * jnp.sqrt(cc / ca) * mixed,
        2.0 * root * mixed,
        square_y + rho * jnp.sqrt(ca / cc) * mixed,
        (1.0 - opaque) * sums[0],
    ] + [sums[6 + c] for c in range(CH)]
    blk[...] = jnp.zeros_like(blk)
    for e in range(SLOTS):
        for v in range(VALS):
            blk[places[e], v : v + 1, :] = out[v][e : e + 1, :]
    lane1 = iota((2, 128), 1)
    group = jnp.where(lane1 // 32 == jnp.bitwise_and(yc, 3), 1.0, 0.0)
    for m in range(12):
        for c in range(CAP):
            pack[m, 10 * c : 10 * c + 10, :] = blk[m * CAP + c, 0:10, :]
        ids = own[m, 30:32, :] if m < 8 else cross[m - 8, 30:32, :]
        pack[m, 30:32, :] = ids * group
    msg_own[...] = pack[0:8].astype(bf16)
    msg_cross[...] = pack[8:12].astype(bf16)


def collect_kernel(got, out):
    lane = iota((1, 128), 1)
    line = lane % 32
    value = jnp.where(line < 10, line, jnp.where(line < 20, line - 10, line - 20))
    goals = []
    for quad in range(8):
        ids = jnp.zeros((1, 128), f32)
        for m in range(4):
            ids = ids + got[quad * 4 + m, 16:32, :].astype(f32)[14:15, :]
        goals.append(jnp.where(line < 30, ids.astype(jnp.int32) + value * BLK_DEV, -1))
    flat = got[...].reshape(32 * MSG, 128)
    rows = 2 * BLK_DEV
    for part in range(VALS // 2):
        here = iota((rows, 128), 0) + part * rows
        hits = [jnp.where(here == goal, 1.0, 0.0).astype(bf16) for goal in goals]
        total = dot(jnp.concatenate(hits, axis=1), flat)
        out[2 * part] = total[:BLK_DEV]
        out[2 * part + 1] = total[BLK_DEV:]


VM = pl.BlockSpec(memory_space=pltpu.VMEM)
SM = pl.BlockSpec(memory_space=pltpu.SMEM)
HB = pl.BlockSpec(memory_space=pltpu.HBM)


def call(kernel, ins, outs, scratch, name, limit=16):
    return pl.pallas_call(
        kernel,
        out_shape=tuple(jax.ShapeDtypeStruct(shape, dtype) for shape, dtype, _ in outs),
        in_specs=ins,
        out_specs=tuple(space for _, _, space in outs),
        scratch_shapes=scratch,
        compiler_params=pltpu.CompilerParams(vmem_limit_bytes=limit << 20 if limit else None),
        name=name,
    )


def on_device(gaussians, target, request, near_counts, render_tile, tile_lists, tile_counts):
    table = constants()
    yc = lax.axis_index("yc")
    wanted = request.transpose(0, 3, 1, 2).reshape(CAP, 1, NEAR)
    n_gs = N_ZQ * N_ZR * N_YC
    up_route = []
    for r in range(n_gs):
        j = r % N_YC
        if j < 4:
            up_route.append((r, (r + N_YC) % n_gs))
        elif j > 4:
            up_route.append((r, (r - N_YC) % n_gs))
    back_route = [(b, a) for a, b in up_route]
    group = N_IMG * N_ZQ
    vm = pltpu.VMEM

    small = [pltpu.SMEM((32,), jnp.int32) for _ in range(3)]
    dma = pltpu.SemaphoreType.DMA

    (sent,) = call(
        pack_kernel,
        [HB, HB],
        [((N_YC, MSG, 128), f32, VM)],
        [pltpu.SMEM((CAP, 1, NEAR), jnp.int32), vm((VALS, BLK_DEV, 128), f32), dma((2,))],
        "pack",
        None,
    )(wanted, gaussians.transpose(1, 0, 2))
    own = lax.all_to_all(sent, "yc", 0, 0, tiled=True)
    own, near_counts, tile_lists, tile_counts, render_tile = lax.optimization_barrier(
        (own, near_counts, tile_lists, tile_counts, render_tile)
    )
    ints = jnp.concatenate(
        [near_counts.reshape(NEAR), tile_lists.reshape(SLOTS), tile_counts.reshape(TILES), render_tile.reshape(TILES)]
    )
    crossing = jnp.where(yc < 4, own[4:8], own[0:4])
    cross = lax.ppermute(crossing, GS, up_route)

    payload, raws, pair_w, beta = call(
        forward_kernel,
        [HB] * 6 + [VM] * 2,
        [
            ((group, 72, 128), bf16, VM),
            ((SLOTS, 16, 128), f32, VM),
            ((PAIRS, PIX, 256), bf16, VM),
            ((PAIRS, PIX, 256), bf16, VM),
        ],
        small
        + [
            vm((CH, SIDE, SIDE), bf16),
            vm((PIX, 32), bf16),
            vm((2, 256, 256), bf16),
            vm((PIX, 128), bf16),
            vm((CH, SIDE, 128), bf16),
            vm((36, 16, 128), f32),
            vm((6, 16, 128), f32),
            vm((PAIRS, 32, 256), f32),
            vm((PAIRS, 16, 256), f32),
            vm((TILES, 8, PIX), f32),
            dma((6,)),
        ],
        "forward",
    )(
        ints, target, table["mom"], table["tri"], table["spread"], table["place"],
        own, cross,
    )
    got = lax.all_to_all(payload, ("img", "zq"), 0, 0, tiled=True)

    up, edge, err_own, rendered = call(
        error_kernel,
        [VM] * 3,
        [
            ((N_ZQ, SIDE, 128), f32, VM),
            ((N_ZQ, SIDE, 128), bf16, VM),
            ((N_ZQ, SIDE, 128), f32, VM),
            ((CH, SIDE, SIDE), bf16, VM),
        ],
        [vm((N_IMG * SIDE, 512), f32), vm((16, SIDE, 128), f32)],
        "error",
    )(got, table["vert"], table["placet"])

    other = [((2 * c - 1) % n_gs, 2 * c) for c in range(n_gs // 2)]
    other = other + [(b, a) for a, b in other]
    got_other = lax.ppermute(edge, GS, other)
    got_mate = lax.ppermute(edge, GS, [(r, r ^ 1) for r in range(n_gs)])

    pixel_grad, msg_own, msg_cross = call(
        backward_kernel,
        [HB] * 6 + [VM] * 9,
        [((CH, SIDE, SIDE), bf16, VM), ((N_YC, MSG, 128), bf16, VM), ((4, MSG, 128), bf16, VM)],
        small
        + [
            vm((3, 768, 128), bf16),
            vm((CH, 128, SIDE), bf16),
            vm((128, PIX), bf16),
            vm((16, PIX), bf16),
            vm((2, 256, 256), bf16),
            vm((128, 256), f32),
            vm((128, 128), f32),
            vm((N_ZQ, SIDE, 128), f32),
            vm((6, 16, 128), f32),
            vm((10, 16, 128), f32),
            vm((36, 16, 128), f32),
            vm((12, MSG, 128), f32),
            vm((PAIRS, 32, 256), f32),
            vm((PAIRS, TILES, 8, 256), f32),
            dma((6,)),
        ],
        "backward",
    )(
        ints, table["horiz"], table["placet"], table["spreadt"], table["momt"],
        table["trib"], up, got_mate, got_other, err_own, raws, pair_w, beta, own, cross,
    )
    returned = lax.ppermute(msg_cross, GS, back_route)
    apart = jnp.arange(N_YC) + NEAR // 2 - yc
    straight = ((apart >= 0) & (apart < NEAR))[:, None, None]
    merged = jnp.where(straight, msg_own, jnp.concatenate([returned, returned], axis=0))
    spread_out = jnp.broadcast_to(merged[None], (N_IMG, N_YC, MSG, 128)).reshape(N_IMG * N_YC, MSG, 128)
    all_msgs = lax.all_to_all(spread_out, ("img", "yc"), 0, 0, tiled=True)
    (summed,) = call(collect_kernel, [VM], [((VALS, BLK_DEV, 128), f32, VM)], [], "collect")(all_msgs)
    return (rendered, pixel_grad, summed.transpose(1, 0, 2))


def solution(mesh):
    wide = Mesh(mesh.devices.reshape(N_IMG, N_ZQ, N_ZR, N_YC), ("img", "zq", "zr", "yc"))
    in_specs = (
        P(GS, None, None),
        P(None, "img", GS),
        P("img", GS, None, None),
        P("img", GS, None),
        P("img", GS, None),
        P("img", GS, None),
        P("img", GS, None),
    )
    out_specs = (P(None, "img", GS), P(None, "img", GS), P(GS, None, None))
    return jax.shard_map(on_device, mesh=wide, in_specs=in_specs, out_specs=out_specs, check_vma=False)
```
